256 devices in a mesh: ens: 8 (over z), dom: 32 (over y, x, core).
Axes of the slice: x: 4, y: 4, z: 8, core: 2. Of those that a mesh axis runs over, the one named last changes fastest.
Arguments:
- state: float32 [256, 1024, 128], P('ens', 'dom'), may hold values from -6 to 6
- row_courant: float32 [1024, 128], P('dom'), may hold values from 0.3 to 0.6
- col_courant: float32 [1024, 128], P('dom'), may hold values from 0.05 to 0.2
- diffusion: float32 [1024, 128], P('dom'), may hold values from 0.01 to 0.05
- obs_values: float32 [4, 256], replicated, may hold values from -8 to 8
- obs_variance: float32 [4, 256], replicated, may hold values from 0.25 to 4
- obs_offsets: int32 [4, 256], replicated, may hold values from 0 to 4095
- owners: int32 [4], replicated, may hold values from 0 to 31, as said below
Outputs:
- analysis: float32 [256, 1024, 128], P('ens', 'dom')
The draws below stay inside these ranges and needn't reach their ends.
Inputs may be any that keep to these rules, and one draw needn't show every extreme that they name: `owners`: distinct domain blocks, one for each batch.
All inputs are finite; a program needn't handle non-finite values.
Results may differ from the reference program's by a relative error of at most 0.0002.
Values sent between devices are 32-bit elements; how exact they have to be, the bound alone decides.
A program may use at most 64 MiB of HBM per device.

```python
import math
import jax
import jax.numpy as jnp
from jax import lax

ROWS_DEV = 32
COLS = 128
NOB = 256
NB = 4
FSTEPS = 4
MEMBERS = 256
ROWS = 1024
N_DOM = 32


def draw_owners(key, part):
    inner_key = jax.random.fold_in(key, 11)
    order_key = jax.random.fold_in(key, 23)
    inner = 1 + jax.random.permutation(inner_key, N_DOM - 2)[:NB - 2]
    ends = jnp.array([0, N_DOM - 1], dtype=jnp.int32)
    values = jnp.concatenate([ends, inner.astype(jnp.int32)])
    order = jax.random.permutation(order_key, NB)
    return values[order].astype(jnp.int32)


def touch_ends(values, key, low, largest):
    longest = values.shape.index(max(values.shape))
    spots = []
    for shift in (0, 1):
        where = [jax.random.randint(jax.random.fold_in(key, axis), (), 0, length) for axis, length in enumerate(values.shape)]
        where[longest] = (where[longest] + shift) % values.shape[longest]
        spots.append(tuple(where))
    return values.at[spots[0]].set(low).at[spots[1]].set(largest)


def steps_of(own_key, dims, cuts, low, top_value):
    def one(axis_at, parts):
        steps = jax.random.uniform(jax.random.fold_in(jax.random.fold_in(own_key, 6), axis_at), (parts,), jnp.float32, low / len(cuts), top_value / len(cuts))
        return jnp.repeat(jnp.exp(steps), dims[axis_at] // parts).reshape((-1,) + (1,) * (len(dims) - axis_at - 1))

    loudness = one(*cuts[0])
    for cut in cuts[1:]:
        loudness = loudness * one(*cut)
    return loudness


def centred(rng, shape, scale, most, pieces=(), kind=jnp.bfloat16):
    gain = steps_of(rng, shape, pieces, -0.22, 0.18) if pieces else 1.0
    drawn = jax.random.normal(rng, shape, jnp.float32) * scale * gain
    return jnp.minimum(jnp.maximum(drawn, -most), most).astype(kind)


def setup_inputs(seed: int = 0) -> dict:
    splits = jax.random.split(jax.random.key(seed), 9)
    return {
        "state": centred(splits[0], (MEMBERS, ROWS, COLS), 1.0, 6.0, ((0, 8), (1, 32)), jnp.float32),
        "row_courant": jnp.clip(0.3 + 0.3 * jax.random.uniform(splits[1], (ROWS, COLS), jnp.float32) ** steps_of(splits[1], (ROWS, COLS), ((0, 32),), -0.2, 0.2), 0.3, 0.6),
        "col_courant": jnp.clip(0.05 + 0.15 * jax.random.uniform(splits[2], (ROWS, COLS), jnp.float32) ** steps_of(splits[2], (ROWS, COLS), ((0, 32),), -0.2, 0.2), 0.05, 0.2),
        "diffusion": jnp.clip(0.01 + 0.04 * jax.random.uniform(splits[3], (ROWS, COLS), jnp.float32) ** steps_of(splits[3], (ROWS, COLS), ((0, 32),), -0.2, 0.2), 0.01, 0.05),
        "obs_values": centred(splits[4], (NB, NOB), 1.5, 8.0, (), jnp.float32),
        "obs_variance": jnp.clip(jnp.exp(jax.random.uniform(splits[5], (NB, NOB), jnp.float32, math.log(0.25), math.log(4.0))), 0.25, 4.0),
        "obs_offsets": touch_ends(jax.random.randint(splits[6], (NB, NOB), 0, ROWS_DEV * COLS), jax.random.fold_in(splits[6], 1), 0, (ROWS_DEV * COLS) - 1).astype(jnp.int32),
        "owners": draw_owners(jax.random.fold_in(splits[8], 71), 0),
    }


def advance(field, row_courant, col_courant, diffusion):
    upper = jnp.roll(field, 1, axis=1)
    lower = jnp.roll(field, -1, axis=1)
    left = jnp.roll(field, 1, axis=2)
    right = jnp.roll(field, -1, axis=2)
    return field - row_courant * (field - upper) - col_courant * (field - left) + diffusion * (upper + lower + left + right - 4.0 * field)

def reference(state, row_courant, col_courant, diffusion, obs_values, obs_variance, obs_offsets, owners):
    field = state
    for step in range(FSTEPS):
        field = advance(field, row_courant, col_courant, diffusion)
    members = field.shape[0]
    matrix = field.reshape(members, ROWS * COLS)
    for batch in range(NB):
        cells = (owners[batch] * (ROWS_DEV * COLS) + obs_offsets[batch]).astype(jnp.int32)
        observed = jnp.take(matrix, cells, axis=1)
        ybar = jnp.mean(observed, axis=0)
        anom_obs = observed - ybar
        system = jnp.dot(anom_obs.T, anom_obs, precision=lax.Precision.HIGHEST) / (members - 1.0)
        system = system + jnp.diag(obs_variance[batch])
        factor = jnp.linalg.cholesky(system)
        target = (obs_values[batch] - ybar)[None, :] - 0.5 * anom_obs
        weights = jax.scipy.linalg.cho_solve((factor, True), target.T).T
        anomaly = matrix - jnp.mean(matrix, axis=0)
        spread = jnp.dot(anom_obs.T, anomaly, precision=lax.Precision.HIGHEST) / (members - 1.0)
        matrix = matrix + jnp.dot(weights, spread, precision=lax.Precision.HIGHEST)
    return matrix.reshape(state.shape)
```

```python
import functools

import jax
import jax.numpy as jnp
from jax import lax
from jax.experimental import pallas as pl
from jax.experimental.pallas import tpu as pltpu
from jax.sharding import PartitionSpec as P

MESH = pl.DeviceIdType.MESH
FSTEPS = 4
HALO = 8
PAD = 8
HIGHEST = lax.Precision.HIGHEST


def dot(a, b, precision=HIGHEST):
    return jnp.dot(a, b, precision=precision, preferred_element_type=jnp.float32)


def dot_nt(a, b):
    return lax.dot_general(
        a, b, (((1,), (1,)), ((), ())), precision=HIGHEST, preferred_element_type=jnp.float32
    )


def split2(x):
    hi = x.astype(jnp.bfloat16)
    lo = (x - hi.astype(jnp.float32)).astype(jnp.bfloat16)
    return hi, lo


def split3(x):
    hi = x.astype(jnp.bfloat16)
    rest = x - hi.astype(jnp.float32)
    mid = rest.astype(jnp.bfloat16)
    lo = (rest - mid.astype(jnp.float32)).astype(jnp.bfloat16)
    return hi, mid, lo


def bdot(a, b):
    return jnp.dot(a, b, preferred_element_type=jnp.float32)


def kernel(
    state, row_c, col_c, diff, obs, var, off, own_v, own_s, out,
    ext, cext, full, lane_hot, row_hot, hx, a_in, b_out, c_src, arrived, prior, pair,
    total, t_own, load_sem, h_send, h_recv, a_send, a_recv, b_send, b_recv,
    c_send, c_recv, g_send, g_recv,
):
    ens_n = lax.axis_size("ens")
    dom_n = lax.axis_size("dom")
    e = lax.axis_index("ens")
    d = lax.axis_index("dom")
    mem_loc, rows_dev, cols = state.shape
    members = mem_loc * ens_n
    nb, nob = obs.shape
    parts = nob // cols

    loads = [
        pltpu.make_async_copy(state, ext.at[:, pl.ds(HALO, rows_dev), :], load_sem.at[0])
    ]
    for i, coef in enumerate((row_c, col_c, diff)):
        loads.append(
            pltpu.make_async_copy(coef, cext.at[i, pl.ds(HALO, rows_dev), :], load_sem.at[1 + i])
        )
    for copy in loads:
        copy.start()

    barrier = pltpu.get_barrier_semaphore()

    def greet_dom(i, carry):
        pl.semaphore_signal(
            barrier, inc=1, device_id=(e, lax.rem(d + i, dom_n)), device_id_type=MESH
        )
        return carry

    def greet_ens(i, carry):
        pl.semaphore_signal(
            barrier, inc=1, device_id=(lax.rem(e + i, ens_n), d), device_id_type=MESH
        )
        return carry

    lax.fori_loop(1, dom_n, greet_dom, 0)
    lax.fori_loop(1, ens_n, greet_ens, 0)
    pl.semaphore_wait(barrier, dom_n - 1 + ens_n - 1)

    down = lax.rem(d + 1, dom_n)
    up = lax.rem(d + dom_n - 1, dom_n)
    halos = []
    for way, (src_row, dst_row, peer) in enumerate(
        ((rows_dev - HALO, 0, down), (0, HALO + rows_dev, up))
    ):
        halos.append(
            pltpu.make_async_remote_copy(
                src_ref=state.at[:, pl.ds(src_row, HALO), :],
                dst_ref=ext.at[:, pl.ds(dst_row, HALO), :],
                send_sem=h_send.at[way * 4],
                recv_sem=h_recv.at[way * 4],
                device_id=(e, peer),
                device_id_type=MESH,
            )
        )
        for i, coef in enumerate((row_c, col_c, diff)):
            halos.append(
                pltpu.make_async_remote_copy(
                    src_ref=coef.at[pl.ds(src_row, HALO), :],
                    dst_ref=cext.at[i, pl.ds(dst_row, HALO), :],
                    send_sem=h_send.at[way * 4 + 1 + i],
                    recv_sem=h_recv.at[way * 4 + 1 + i],
                    device_id=(e, peer),
                    device_id_type=MESH,
                )
            )
    for copy in halos:
        copy.start()

    mine = (own_v[...] == d).astype(jnp.int32)
    offs = jnp.sum(off[...] * mine, axis=0, keepdims=True)
    lane_of = lax.rem(offs, cols)
    row_of = lax.div(offs, cols)
    lane_hot[...] = (
        lax.broadcasted_iota(jnp.int32, (cols, nob), 0) == lane_of
    ).astype(jnp.float32).astype(jnp.bfloat16)
    row_hot[...] = (
        lax.broadcasted_iota(jnp.int32, (rows_dev, nob), 0) == row_of
    ).astype(jnp.float32)

    for copy in loads:
        copy.wait()
    for copy in halos:
        copy.wait_recv()

    high = rows_dev + 2 * HALO
    rc, cc, df = cext[0], cext[1], cext[2]
    w_up = rc + df
    w_left = cc + df
    w_mid = 1.0 - rc - cc - 4.0 * df
    group = 2

    def forecast(i, carry):
        fields = []
        for j in range(group):
            m = i * group + j
            x = ext[m]
            for _ in range(FSTEPS):
                above = pltpu.roll(x, 1, 0)
                below = pltpu.roll(x, high - 1, 0)
                left = pltpu.roll(x, 1, 1)
                right = pltpu.roll(x, cols - 1, 1)
                x = w_mid * x + w_up * above + w_left * left + df * (below + right)
            x = x[HALO : HALO + rows_dev]
            full[e, pl.ds(m, rows_dev, stride=mem_loc), :] = x
            fields.append(x)
        hi, mid, lo = split3(jnp.concatenate(fields, axis=0))
        hot = lane_hot[...]
        picked = bdot(hi, hot) + bdot(mid, hot) + bdot(lo, hot)
        for j in range(group):
            part = picked[j * rows_dev : (j + 1) * rows_dev] * row_hot[...]
            hx[i * group + j] = jnp.sum(part, axis=0, keepdims=True)
        return carry

    lax.fori_loop(0, mem_loc // group, forecast, 0)

    def a_copy(src, dst, peer):
        return pltpu.make_async_remote_copy(
            src_ref=hx.at[src],
            dst_ref=a_in.at[dst],
            send_sem=a_send.at[peer],
            recv_sem=a_recv.at[dst],
            device_id=(e, peer),
            device_id_type=MESH,
        )

    def a_start(i, carry):
        peer = lax.rem(d + i, dom_n)
        a_copy(peer, d, peer).start()
        return carry

    def a_wait(i, carry):
        peer = lax.rem(d + i, dom_n)
        a_copy(peer, peer, peer).wait_recv()
        return carry

    lax.fori_loop(1, dom_n, a_start, 0)
    a_in[d] = hx[d]

    half = rows_dev * mem_loc // 2
    counts = {
        (0, 0): ens_n // 2,
        (1, 0): (ens_n - 1) // 2,
        (0, 1): (ens_n - 1) // 2,
        (1, 1): ens_n // 2,
    }

    def g_copy(way, part, step, arriving):
        shift = step + 1 if arriving else step
        block = lax.rem(e - shift + ens_n, ens_n) if way == 0 else lax.rem(e + shift, ens_n)
        peer = lax.rem(e + 1, ens_n) if way == 0 else lax.rem(e + ens_n - 1, ens_n)
        where = full.at[block, pl.ds(part * half, half), :]
        slot = (way * 2 + part) * (ens_n // 2) + step
        return pltpu.make_async_remote_copy(
            src_ref=where,
            dst_ref=where,
            send_sem=g_send.at[slot],
            recv_sem=g_recv.at[slot],
            device_id=(peer, d),
            device_id_type=MESH,
        )

    g_started = []

    def g_start(part, step):
        for way in (0, 1):
            if step > 0 and step - 1 < counts[way, part]:
                g_copy(way, part, step - 1, True).wait_recv()
            if step < counts[way, part]:
                g_copy(way, part, step, False).start()
                g_started.append((way, part, step))

    services = [(p, s) for s in range(1, ens_n // 2 + 1) for p in (0, 1)]

    def service():
        if services:
            g_start(*services.pop(0))

    lax.fori_loop(1, dom_n, a_wait, 0)

    for b in range(nb):
        row = a_in[own_s[b]]
        for p in range(parts):
            piece = row[:, p * cols : (p + 1) * cols]
            b_out[b, p] = piece
            c_src[b, p, pl.ds(e, 1), :] = piece

    def b_copy(slot, peer):
        return pltpu.make_async_remote_copy(
            src_ref=b_out,
            dst_ref=c_src.at[:, :, pl.ds(slot, 1), :],
            send_sem=b_send.at[peer],
            recv_sem=b_recv.at[slot],
            device_id=(peer, d),
            device_id_type=MESH,
        )

    def b_start(i, carry):
        peer = lax.rem(e + i, ens_n)
        b_copy(e, peer).start()
        return carry

    def b_wait(i, carry):
        peer = lax.rem(e + i, ens_n)
        b_copy(peer, peer).wait_recv()
        return carry

    lax.fori_loop(1, ens_n, b_start, 0)
    g_start(0, 0)
    g_start(1, 0)
    lax.fori_loop(1, ens_n, b_wait, 0)

    spans = ((0, 1), (1, nb - 1))

    def c_copy(part, slot, peer):
        first, count = spans[part]
        return pltpu.make_async_remote_copy(
            src_ref=c_src.at[pl.ds(first, count)],
            dst_ref=arrived.at[
                pl.ds(first, count), :, pl.ds(pl.multiple_of(slot * ens_n, ens_n), ens_n), :
            ],
            send_sem=c_send.at[part * dom_n + peer],
            recv_sem=c_recv.at[part * dom_n + slot],
            device_id=(e, peer),
            device_id_type=MESH,
        )

    def c_start(part):
        def one(i, carry):
            peer = lax.rem(d + i, dom_n)
            c_copy(part, d, peer).start()
            return carry

        lax.fori_loop(1, dom_n, one, 0)

    def c_wait(part):
        def one(i, carry):
            peer = lax.rem(d + i, dom_n)
            c_copy(part, peer, peer).wait_recv()
            return carry

        lax.fori_loop(1, dom_n, one, 0)

    c_start(0)
    c_start(1)
    arrived[:, :, pl.ds(pl.multiple_of(d * ens_n, ens_n), ens_n), :] = c_src[...]
    service()
    c_wait(0)
    service()

    def in_order(b):
        columns = [
            jnp.concatenate(
                [arrived.at[b, p][pl.ds(k, mem_loc, stride=ens_n), :] for k in range(ens_n)], axis=0
            )
            for p in range(parts)
        ]
        return jnp.concatenate(columns, axis=1)

    eye = (
        lax.broadcasted_iota(jnp.int32, (members, members), 0)
        == lax.broadcasted_iota(jnp.int32, (members, members), 1)
    ).astype(jnp.float32)
    scale = 1.0 / (members - 1.0)
    low = members + PAD

    def analyse(observed, b):
        ybar = jnp.sum(observed, axis=0, keepdims=True) * (1.0 / members)
        rs = 1.0 / jnp.sqrt(var[pl.ds(b, 1), :])
        anom = (observed - ybar) * rs
        innov = (obs[pl.ds(b, 1), :] - ybar) * rs
        left = jnp.concatenate([anom, jnp.broadcast_to(innov, (PAD, nob))], axis=0)
        both = dot_nt(left, anom) * scale
        gram = both[:members]
        z = both[members:]
        size = 1.001 * jnp.sqrt(jnp.sum(gram * gram, keepdims=True))
        alpha = 2.0 / (2.0 + size)
        r = size / (2.0 + size)
        k_mat = eye + gram
        err = eye - alpha * k_mat
        a = 2.0 / (2.0 - r * r)
        first = a * alpha
        pair[:members] = first * (eye + err)
        pair[members:low] = first * (z + dot(z, err))
        pair[low:] = a * dot(err, err) - (a - 1.0) * eye

        def step(i, r):
            a = 2.0 / (2.0 - r * r)
            held = pair[...]
            prod = dot(held, held[low:])
            pair[:low] = a * (held[:low] + prod[:low])
            pair[low:] = a * prod[low:] - (a - 1.0) * eye
            return a - 1.0

        r = lax.fori_loop(0, 7, step, a - 1.0)
        a = 2.0 / (2.0 - r * r)
        x = pair[:low]
        x = a * (x + dot(x, pair[low:]))
        for _ in range(2):
            x = x + dot(x, eye - dot(k_mat, x[:members]))
        return x

    def update(x, columns):
        prod = dot(x, columns)
        return 0.5 * (columns + prod[:members]) + prod[members : members + 1]

    observed = in_order(0)
    for b in range(nb):
        x = analyse(observed, b)
        service()
        if b == 0:
            c_wait(1)
            total[...] = 0.5 * (eye + x[:members]) + x[members : members + 1]
            for later in range(1, nb):
                fresh = update(x, in_order(later))
                if later == 1:
                    observed = fresh
                else:
                    prior[later] = fresh
        elif b < nb - 1:
            for later in range(b + 1, nb):
                fresh = update(x, prior[later])
                if later == b + 1:
                    observed = fresh
                else:
                    prior[later] = fresh
            total[...] = update(x, total[...])
        else:
            pair[:low] = x
            rows = pl.ds(pl.multiple_of(e * mem_loc, mem_loc), mem_loc)
            thin = jnp.concatenate([pair[rows], x[members:]], axis=0)
            prod = dot(thin, total[...])
            t_own[...] = (
                0.5 * (total[rows] + prod[:mem_loc]) + prod[mem_loc : mem_loc + 1]
            )

    while services:
        service()

    hi, lo = split2(t_own[...])
    both = jnp.concatenate([hi, lo], axis=0)

    def apply(i, carry):
        pieces = [
            jnp.concatenate(
                [
                    full[k, pl.ds(pl.multiple_of((2 * i + j) * mem_loc, mem_loc), mem_loc), :]
                    for k in range(ens_n)
                ],
                axis=0,
            )
            for j in range(2)
        ]
        x_hi, x_lo = split2(jnp.concatenate(pieces, axis=1))
        one = bdot(both, x_hi)
        res = one[:mem_loc] + one[mem_loc:] + bdot(hi, x_lo)
        out[pl.ds(2 * i, mem_loc, stride=rows_dev), :] = res[:, :cols]
        out[pl.ds(2 * i + 1, mem_loc, stride=rows_dev), :] = res[:, cols:]
        return carry

    lax.fori_loop(0, rows_dev // 2, apply, 0)

    for copy in halos:
        copy.wait_send()
    for way, part, step in g_started:
        g_copy(way, part, step, False).wait_send()

    def sent_dom(i, carry):
        peer = lax.rem(d + i, dom_n)
        a_copy(peer, d, peer).wait_send()
        c_copy(0, d, peer).wait_send()
        c_copy(1, d, peer).wait_send()
        return carry

    def sent_ens(i, carry):
        b_copy(e, lax.rem(e + i, ens_n)).wait_send()
        return carry

    lax.fori_loop(1, dom_n, sent_dom, 0)
    lax.fori_loop(1, ens_n, sent_ens, 0)


def on_device(mesh_shape, state, row_c, col_c, diff, obs, var, off, owners):
    ens_n, dom_n = mesh_shape
    mem_loc, rows_dev, cols = state.shape
    members = mem_loc * ens_n
    nb, nob = obs.shape
    high = rows_dev + 2 * HALO
    f32 = jnp.float32
    sem = pltpu.SemaphoreType.DMA
    slots = 4 * (ens_n // 2)
    hbm = pl.BlockSpec(memory_space=pl.ANY)
    vmem = pl.BlockSpec(memory_space=pltpu.VMEM)
    result = pl.pallas_call(
        kernel,
        out_shape=jax.ShapeDtypeStruct((mem_loc * rows_dev, cols), f32),
        in_specs=[hbm, hbm, hbm, hbm, vmem, vmem, vmem, vmem, pl.BlockSpec(memory_space=pltpu.SMEM)],
        out_specs=vmem,
        scratch_shapes=[
            pltpu.VMEM((mem_loc, high, cols), f32),
            pltpu.VMEM((3, high, cols), f32),
            pltpu.VMEM((ens_n, rows_dev * mem_loc, cols), f32),
            pltpu.VMEM((cols, nob), jnp.bfloat16),
            pltpu.VMEM((rows_dev, nob), f32),
            pltpu.VMEM((mem_loc, 1, nob), f32),
            pltpu.VMEM((dom_n, 1, nob), f32),
            pltpu.VMEM((nb, nob // cols, 1, cols), f32),
            pltpu.VMEM((nb, nob // cols, ens_n, cols), f32),
            pltpu.VMEM((nb, nob // cols, members, cols), f32),
            pltpu.VMEM((nb, members, nob), f32),
            pltpu.VMEM((2 * members + PAD, members), f32),
            pltpu.VMEM((members, members), f32),
            pltpu.VMEM((mem_loc, members), f32),
            sem((4,)),
            sem((8,)),
            sem((8,)),
            sem((dom_n,)),
            sem((dom_n,)),
            sem((ens_n,)),
            sem((ens_n,)),
            sem((2 * dom_n,)),
            sem((2 * dom_n,)),
            sem((slots,)),
            sem((slots,)),
        ],
        compiler_params=pltpu.CompilerParams(
            collective_id=0, has_side_effects=True, vmem_limit_bytes=48 * 1024 * 1024
        ),
    )(state, row_c, col_c, diff, obs, var, off, owners.reshape(nb, 1), owners)
    return result.reshape(mem_loc, rows_dev, cols)


def solution(mesh):
    sizes = (mesh.shape["ens"], mesh.shape["dom"])
    return jax.shard_map(
        functools.partial(on_device, sizes),
        mesh=mesh,
        in_specs=(
            P("ens", "dom", None),
            P("dom", None),
            P("dom", None),
            P("dom", None),
            P(),
            P(),
            P(),
            P(),
        ),
        out_specs=P("ens", "dom", None),
        check_vma=False,
    )
```

```python
import functools

import jax
import jax.numpy as jnp
from jax import lax
from jax.experimental import pallas as pl
from jax.experimental.pallas import tpu as pltpu
from jax.sharding import PartitionSpec as P

MESH = pl.DeviceIdType.MESH
FSTEPS = 4
HALO = 8
PAD = 8
HIGHEST = lax.Precision.HIGHEST


def dot(a, b, precision=HIGHEST):
    return jnp.dot(a, b, precision=precision, preferred_element_type=jnp.float32)


def dot_nt(a, b):
    return lax.dot_general(
        a, b, (((1,), (1,)), ((), ())), precision=HIGHEST, preferred_element_type=jnp.float32
    )


def split2(x):
    hi = x.astype(jnp.bfloat16)
    lo = (x - hi.astype(jnp.float32)).astype(jnp.bfloat16)
    return hi, lo


def bdot(a, b):
    return jnp.dot(a, b, preferred_element_type=jnp.float32)


def dot3(a, b):
    a_hi, a_lo = a
    b_hi, b_lo = b
    return bdot(
        jnp.concatenate([a_hi, a_lo, a_hi], axis=1), jnp.concatenate([b_hi, b_hi, b_lo], axis=0)
    )


def kernel(
    state, row_c, col_c, diff, obs_in, var_in, off_in, own_in, out,
    ext, cext, cells, weight, full, obs, var, off, own, lane_hot, row_hot, hx, a_in, b_out, c_src,
    arrived, prior, pair, gram_s, total, t_own,
    load_sem, h_send, h_recv, a_send, a_recv, b_send, b_recv, c_send, c_recv, g_send, g_recv,
):
    ens_n = lax.axis_size("ens")
    dom_n = lax.axis_size("dom")
    e = lax.axis_index("ens")
    d = lax.axis_index("dom")
    mem_loc, rows_dev, cols = state.shape
    members = mem_loc * ens_n
    nb, nob = obs.shape
    parts = nob // cols
    high = rows_dev + 2 * HALO

    inner = pl.ds(HALO, rows_dev)
    moves = [(state, ext.at[:, inner, :])]
    moves += [(coef, cext.at[i, inner, :]) for i, coef in enumerate((row_c, col_c, diff))]
    moves += [(obs_in, obs), (var_in, var), (off_in, off), (own_in, own)]
    loads = [pltpu.make_async_copy(src, dst, load_sem.at[i]) for i, (src, dst) in enumerate(moves)]
    for copy in loads:
        copy.start()

    barrier = pltpu.get_barrier_semaphore()

    def greet_dom(i, carry):
        pl.semaphore_signal(
            barrier, inc=1, device_id=(e, lax.rem(d + i, dom_n)), device_id_type=MESH
        )
        return carry

    def greet_ens(i, carry):
        pl.semaphore_signal(
            barrier, inc=1, device_id=(lax.rem(e + i, ens_n), d), device_id_type=MESH
        )
        return carry

    lax.fori_loop(1, dom_n, greet_dom, 0)
    lax.fori_loop(1, ens_n, greet_ens, 0)
    pl.semaphore_wait(barrier, dom_n - 1 + ens_n - 1)

    down = lax.rem(d + 1, dom_n)
    up = lax.rem(d + dom_n - 1, dom_n)
    halos = []
    for way, (src_row, dst_row, peer) in enumerate(
        ((rows_dev - HALO, 0, down), (0, HALO + rows_dev, up))
    ):
        halos.append(
            pltpu.make_async_remote_copy(
                src_ref=state.at[:, pl.ds(src_row, HALO), :],
                dst_ref=ext.at[:, pl.ds(dst_row, HALO), :],
                send_sem=h_send.at[way * 4],
                recv_sem=h_recv.at[way * 4],
                device_id=(e, peer),
                device_id_type=MESH,
            )
        )
        for i, coef in enumerate((row_c, col_c, diff)):
            halos.append(
                pltpu.make_async_remote_copy(
                    src_ref=coef.at[pl.ds(src_row, HALO), :],
                    dst_ref=cext.at[i, pl.ds(dst_row, HALO), :],
                    send_sem=h_send.at[way * 4 + 1 + i],
                    recv_sem=h_recv.at[way * 4 + 1 + i],
                    device_id=(e, peer),
                    device_id_type=MESH,
                )
            )
    for copy in halos:
        copy.start()

    for copy in loads:
        copy.wait()

    offs = jnp.zeros((1, nob), jnp.int32)
    for b in range(nb):
        offs = offs + off[pl.ds(b, 1), :] * (own[b] == d).astype(jnp.int32)
    lane_of = lax.rem(offs, cols)
    row_of = lax.div(offs, cols)
    lane_hot[...] = (
        lax.broadcasted_iota(jnp.int32, (cols, nob), 0) == lane_of
    ).astype(jnp.float32).astype(jnp.bfloat16)
    row_hot[...] = (
        lax.broadcasted_iota(jnp.int32, (rows_dev, nob), 0) == row_of
    ).astype(jnp.float32)

    def turn(first, count):
        def one(m, carry):
            cells[pl.ds(first * mem_loc + m, count, stride=mem_loc), :] = ext[m, pl.ds(first, count), :]
            return carry

        lax.fori_loop(0, mem_loc, one, 0, unroll=4)

    turn(HALO, rows_dev)
    for copy in halos:
        copy.wait_recv()
    turn(0, HALO)
    turn(HALO + rows_dev, HALO)
    rc, cc, df = cext[0], cext[1], cext[2]
    weight[0] = 1.0 - rc - cc - 4.0 * df
    weight[1] = rc + df
    weight[2] = cc + df
    weight[3] = df

    def at_row(r):
        return pl.ds(pl.multiple_of(r * mem_loc, mem_loc), mem_loc)

    def coef(i, r):
        return jnp.broadcast_to(weight[i, pl.ds(r, 1), :], (mem_loc, cols))

    for step in range(FSTEPS):
        first = HALO - (FSTEPS - 1 - step)
        last = HALO + rows_dev + (FSTEPS - 1 - step)

        def one(r, carry, step=step):
            above, here = carry
            below = cells[at_row(r + 1), :]
            left = pltpu.roll(here, 1, 1)
            right = pltpu.roll(here, cols - 1, 1)
            fresh = (
                coef(0, r) * here
                + coef(1, r) * above
                + coef(2, r) * left
                + coef(3, r) * (below + right)
            )
            if step < FSTEPS - 1:
                cells[at_row(r), :] = fresh
            else:
                full[e, at_row(r - HALO), :] = fresh
            return here, below

        lax.fori_loop(
            first, last, one, (cells[at_row(first - 1), :], cells[at_row(first), :]), unroll=4
        )

    half = rows_dev * mem_loc // 2

    def g_copy(way, part, step, arriving):
        shift = step + 1 if arriving else step
        block = lax.rem(e - shift + ens_n, ens_n) if way == 0 else lax.rem(e + shift, ens_n)
        peer = lax.rem(e + 1, ens_n) if way == 0 else lax.rem(e + ens_n - 1, ens_n)
        where = full.at[block, pl.ds(pl.multiple_of(part * half, half), half), :]
        slot = (way * 2 + part) * 4 + step
        return pltpu.make_async_remote_copy(
            src_ref=where,
            dst_ref=where,
            send_sem=g_send.at[slot],
            recv_sem=g_recv.at[slot],
            device_id=(peer, d),
            device_id_type=MESH,
        )

    def g_start(part, step):
        for way in (0, 1):
            g_copy(way, part, step, False).start()

    def g_wait(part, step):
        for way in (0, 1):
            g_copy(way, part, step, True).wait_recv()

    g_start(0, 0)

    rows_once = 4

    def pick(i, acc):
        block = pl.ds(pl.multiple_of(i * rows_once * mem_loc, rows_once * mem_loc), rows_once * mem_loc)
        hi, lo = split2(full[e, block, :])
        hot = lane_hot[...]
        picked = bdot(hi, hot) + bdot(lo, hot)
        for j in range(rows_once):
            acc = acc + picked[j * mem_loc : (j + 1) * mem_loc] * row_hot[
                pl.ds(i * rows_once + j, 1), :
            ]
        return acc

    hx[...] = lax.fori_loop(
        0, rows_dev // rows_once, pick, jnp.zeros((mem_loc, nob), jnp.float32), unroll=2
    )

    def a_copy(src, dst, peer):
        return pltpu.make_async_remote_copy(
            src_ref=hx.at[pl.ds(src, 1), :],
            dst_ref=a_in.at[dst],
            send_sem=a_send.at[peer],
            recv_sem=a_recv.at[dst],
            device_id=(e, peer),
            device_id_type=MESH,
        )

    def a_start(i, carry):
        peer = lax.rem(d + i, dom_n)
        a_copy(peer, d, peer).start()
        return carry

    def a_wait(i, carry):
        peer = lax.rem(d + i, dom_n)
        a_copy(peer, peer, peer).wait_recv()
        return carry

    lax.fori_loop(1, dom_n, a_start, 0)
    a_in[d] = hx[pl.ds(d, 1), :]

    lax.fori_loop(1, dom_n, a_wait, 0)

    for b in range(nb):
        row = a_in[own[b]]
        for p in range(parts):
            piece = row[:, p * cols : (p + 1) * cols]
            b_out[b, p] = piece
            c_src[b, p, pl.ds(e, 1), :] = piece

    def b_copy(slot, peer):
        return pltpu.make_async_remote_copy(
            src_ref=b_out,
            dst_ref=c_src.at[:, :, pl.ds(slot, 1), :],
            send_sem=b_send.at[peer],
            recv_sem=b_recv.at[slot],
            device_id=(peer, d),
            device_id_type=MESH,
        )

    def b_start(i, carry):
        peer = lax.rem(e + i, ens_n)
        b_copy(e, peer).start()
        return carry

    def b_wait(i, carry):
        peer = lax.rem(e + i, ens_n)
        b_copy(peer, peer).wait_recv()
        return carry

    lax.fori_loop(1, ens_n, b_start, 0)
    g_start(1, 0)
    lax.fori_loop(1, ens_n, b_wait, 0)

    spans = ((0, 1), (1, nb - 1))

    def c_copy(part, slot, peer):
        first, count = spans[part]
        return pltpu.make_async_remote_copy(
            src_ref=c_src.at[pl.ds(first, count)],
            dst_ref=arrived.at[
                pl.ds(first, count), :, pl.ds(pl.multiple_of(slot * ens_n, ens_n), ens_n), :
            ],
            send_sem=c_send.at[part * dom_n + peer],
            recv_sem=c_recv.at[part * dom_n + slot],
            device_id=(e, peer),
            device_id_type=MESH,
        )

    def c_start(part):
        def one(i, carry):
            peer = lax.rem(d + i, dom_n)
            c_copy(part, d, peer).start()
            return carry

        lax.fori_loop(1, dom_n, one, 0)

    def c_wait(part):
        def one(i, carry):
            peer = lax.rem(d + i, dom_n)
            c_copy(part, peer, peer).wait_recv()
            return carry

        lax.fori_loop(1, dom_n, one, 0)

    c_start(0)
    c_start(1)
    g_wait(0, 0)
    g_start(0, 1)
    arrived[:, :, pl.ds(pl.multiple_of(d * ens_n, ens_n), ens_n), :] = c_src[...]
    c_wait(0)
    g_wait(1, 0)
    g_start(1, 1)

    def in_order(b):
        columns = [
            jnp.concatenate(
                [arrived.at[b, p][pl.ds(k, mem_loc, stride=ens_n), :] for k in range(ens_n)], axis=0
            )
            for p in range(parts)
        ]
        return jnp.concatenate(columns, axis=1)

    eye = (
        lax.broadcasted_iota(jnp.int32, (members, members), 0)
        == lax.broadcasted_iota(jnp.int32, (members, members), 1)
    ).astype(jnp.float32)
    scale = 1.0 / (members - 1.0)
    low = members + PAD

    def analyse(observed, b):
        ybar = jnp.sum(observed, axis=0, keepdims=True) * (1.0 / members)
        rs = 1.0 / jnp.sqrt(var[pl.ds(b, 1), :])
        anom = (observed - ybar) * rs
        innov = (obs[pl.ds(b, 1), :] - ybar) * rs
        left = jnp.concatenate([anom, jnp.broadcast_to(innov, (PAD, nob))], axis=0)
        both = dot_nt(left, anom) * scale
        gram = both[:members]
        z = both[members:]
        size = 1.001 * jnp.sqrt(jnp.sum(gram * gram, keepdims=True))
        alpha = 2.0 / (2.0 + size)
        r = size / (2.0 + size)
        k_mat = eye + gram
        gram_s[...] = k_mat
        err = eye - alpha * k_mat
        a = 2.0 / (2.0 - r * r)
        prod = dot(jnp.concatenate([z, err], axis=0), err)
        first = a * alpha
        pair[:members] = first * (eye + err)
        pair[members:low] = first * (z + prod[:PAD])
        pair[low:] = a * prod[PAD:] - (a - 1.0) * eye

        def step(i, r):
            a = 2.0 / (2.0 - r * r)
            held = pair[...]
            hi, lo = split2(held)
            prod = dot3((hi, lo), (hi[low:], lo[low:]))
            pair[:low] = a * (held[:low] + prod[:low])
            pair[low:] = a * prod[low:] - (a - 1.0) * eye
            return a - 1.0

        r = lax.fori_loop(0, 7, step, a - 1.0)
        a = 2.0 / (2.0 - r * r)
        x = pair[:low]
        x = a * (x + dot3(split2(x), split2(pair[low:])))
        pair[:low] = x

        def correct(i, carry):
            x = pair[:low]
            rest = eye - dot(gram_s[...], x[:members])
            pair[:low] = x + dot3(split2(x), split2(rest))
            return carry

        lax.fori_loop(0, 2, correct, 0)
        x = pair[:low]
        want = (lax.broadcasted_iota(jnp.int32, (low, 1), 0) < members).astype(jnp.float32)
        return x + (want - jnp.sum(x, axis=1, keepdims=True)) * (1.0 / members)

    def update(x, columns):
        prod = dot3(x, split2(columns))
        return 0.5 * (columns + prod[:members]) + prod[members : members + 1]

    prior[0] = in_order(0)
    total[...] = eye

    def batch(b, carry):
        x = split2(analyse(prior[b], b))

        @pl.when(b == 0)
        def _():
            c_wait(1)
            for later in range(1, nb):
                prior[later] = in_order(later)

        def later_one(later, carry):
            prior[later] = update(x, prior[later])
            return carry

        lax.fori_loop(b + 1, nb, later_one, 0)
        total[...] = update(x, total[...])
        part = lax.rem(b, 2)
        step = 2 + lax.div(b, 2)
        g_wait(part, step - 1)
        for way in (0, 1):

            @pl.when((b < 2) | (part == way))
            def _():
                g_copy(way, part, step, False).start()

        return carry

    lax.fori_loop(0, nb, batch, 0)
    rows = pl.ds(pl.multiple_of(e * mem_loc, mem_loc), mem_loc)
    t_own[...] = total[rows, :]
    g_copy(0, 0, 3, True).wait_recv()
    g_copy(1, 1, 3, True).wait_recv()

    hi, lo = split2(t_own[...])
    both = jnp.concatenate([hi, lo], axis=0)

    def apply(i, carry):
        pieces = [
            jnp.concatenate(
                [
                    full[k, pl.ds(pl.multiple_of((2 * i + j) * mem_loc, mem_loc), mem_loc), :]
                    for k in range(ens_n)
                ],
                axis=0,
            )
            for j in range(2)
        ]
        x_hi, x_lo = split2(jnp.concatenate(pieces, axis=1))
        one = bdot(both, x_hi)
        res = one[:mem_loc] + one[mem_loc:] + bdot(hi, x_lo)
        out[pl.ds(2 * i, mem_loc, stride=rows_dev), :] = res[:, :cols]
        out[pl.ds(2 * i + 1, mem_loc, stride=rows_dev), :] = res[:, cols:]
        return carry

    lax.fori_loop(0, rows_dev // 2, apply, 0)

    for copy in halos:
        copy.wait_send()
    for way in (0, 1):
        for part in (0, 1):
            for step in range(4 if way == part else 3):
                g_copy(way, part, step, False).wait_send()

    def sent_dom(i, carry):
        peer = lax.rem(d + i, dom_n)
        a_copy(peer, d, peer).wait_send()
        c_copy(0, d, peer).wait_send()
        c_copy(1, d, peer).wait_send()
        return carry

    def sent_ens(i, carry):
        b_copy(e, lax.rem(e + i, ens_n)).wait_send()
        return carry

    lax.fori_loop(1, dom_n, sent_dom, 0)
    lax.fori_loop(1, ens_n, sent_ens, 0)


def on_device(mesh_shape, state, row_c, col_c, diff, obs, var, off, owners):
    ens_n, dom_n = mesh_shape
    mem_loc, rows_dev, cols = state.shape
    members = mem_loc * ens_n
    nb, nob = obs.shape
    high = rows_dev + 2 * HALO
    f32 = jnp.float32
    sem = pltpu.SemaphoreType.DMA
    assert ens_n == 8 and nb == 4
    hbm = pl.BlockSpec(memory_space=pl.ANY)
    vmem = pl.BlockSpec(memory_space=pltpu.VMEM)
    result = pl.pallas_call(
        kernel,
        out_shape=jax.ShapeDtypeStruct((mem_loc * rows_dev, cols), f32),
        in_specs=[hbm] * 8,
        out_specs=vmem,
        scratch_shapes=[
            pltpu.VMEM((mem_loc, high, cols), f32),
            pltpu.VMEM((3, high, cols), f32),
            pltpu.VMEM((high * mem_loc, cols), f32),
            pltpu.VMEM((4, high, cols), f32),
            pltpu.VMEM((ens_n, rows_dev * mem_loc, cols), f32),
            pltpu.VMEM((nb, nob), f32),
            pltpu.VMEM((nb, nob), f32),
            pltpu.VMEM((nb, nob), jnp.int32),
            pltpu.SMEM((nb,), jnp.int32),
            pltpu.VMEM((cols, nob), jnp.bfloat16),
            pltpu.VMEM((rows_dev, nob), f32),
            pltpu.VMEM((mem_loc, nob), f32),
            pltpu.VMEM((dom_n, 1, nob), f32),
            pltpu.VMEM((nb, nob // cols, 1, cols), f32),
            pltpu.VMEM((nb, nob // cols, ens_n, cols), f32),
            pltpu.VMEM((nb, nob // cols, members, cols), f32),
            pltpu.VMEM((nb, members, nob), f32),
            pltpu.VMEM((2 * members + PAD, members), f32),
            pltpu.VMEM((members, members), f32),
            pltpu.VMEM((members, members), f32),
            pltpu.VMEM((mem_loc, members), f32),
            sem((8,)),
            sem((8,)),
            sem((8,)),
            sem((dom_n,)),
            sem((dom_n,)),
            sem((ens_n,)),
            sem((ens_n,)),
            sem((2 * dom_n,)),
            sem((2 * dom_n,)),
            sem((16,)),
            sem((16,)),
        ],
        compiler_params=pltpu.CompilerParams(
            collective_id=0, has_side_effects=True, vmem_limit_bytes=60 * 1024 * 1024
        ),
    )(state, row_c, col_c, diff, obs, var, off, owners)
    return result.reshape(mem_loc, rows_dev, cols)


def solution(mesh):
    sizes = (mesh.shape["ens"], mesh.shape["dom"])
    return jax.shard_map(
        functools.partial(on_device, sizes),
        mesh=mesh,
        in_specs=(
            P("ens", "dom", None),
            P("dom", None),
            P("dom", None),
            P("dom", None),
            P(),
            P(),
            P(),
            P(),
        ),
        out_specs=P("ens", "dom", None),
        check_vma=False,
    )
```

```python
import functools

import jax
import jax.numpy as jnp
from jax import lax
from jax.experimental import pallas as pl
from jax.experimental.pallas import tpu as pltpu
from jax.sharding import PartitionSpec as P

MESH = pl.DeviceIdType.MESH
FSTEPS = 4
HALO = 8
PAD = 8
HIGHEST = lax.Precision.HIGHEST


def dot(a, b, precision=HIGHEST):
    return jnp.dot(a, b, precision=precision, preferred_element_type=jnp.float32)


def dot_nt(a, b):
    return lax.dot_general(
        a, b, (((1,), (1,)), ((), ())), precision=HIGHEST, preferred_element_type=jnp.float32
    )


def split2(x):
    hi = x.astype(jnp.bfloat16)
    lo = (x - hi.astype(jnp.float32)).astype(jnp.bfloat16)
    return hi, lo


def bdot(a, b):
    return jnp.dot(a, b, preferred_element_type=jnp.float32)


def dot3(a, b):
    a_hi, a_lo = a
    b_hi, b_lo = b
    return bdot(
        jnp.concatenate([a_hi, a_lo, a_hi], axis=1), jnp.concatenate([b_hi, b_hi, b_lo], axis=0)
    )


def kernel(
    state, row_c, col_c, diff, obs_in, var_in, off_in, own_in, out,
    ext, cext, cells, other, weight, full, obs, var, off, own, lane_hot, row_hot, hx, a_in, b_out, c_src,
    arrived, prior, pair, gram_s, total, t_own,
    load_sem, h_send, h_recv, a_send, a_recv, b_send, b_recv, c_send, c_recv, g_send, g_recv,
):
    ens_n = lax.axis_size("ens")
    dom_n = lax.axis_size("dom")
    e = lax.axis_index("ens")
    d = lax.axis_index("dom")
    mem_loc, rows_dev, cols = state.shape
    members = mem_loc * ens_n
    nb, nob = obs.shape
    parts = nob // cols
    high = rows_dev + 2 * HALO

    inner = pl.ds(HALO, rows_dev)
    moves = [(state, ext.at[:, inner, :])]
    moves += [(coef, cext.at[i, inner, :]) for i, coef in enumerate((row_c, col_c, diff))]
    moves += [(obs_in, obs), (var_in, var), (off_in, off), (own_in, own)]
    loads = [pltpu.make_async_copy(src, dst, load_sem.at[i]) for i, (src, dst) in enumerate(moves)]
    for copy in loads:
        copy.start()

    barrier = pltpu.get_barrier_semaphore()

    def greet_dom(i, carry):
        pl.semaphore_signal(
            barrier, inc=1, device_id=(e, lax.rem(d + i, dom_n)), device_id_type=MESH
        )
        return carry

    def greet_ens(i, carry):
        pl.semaphore_signal(
            barrier, inc=1, device_id=(lax.rem(e + i, ens_n), d), device_id_type=MESH
        )
        return carry

    lax.fori_loop(1, dom_n, greet_dom, 0)
    lax.fori_loop(1, ens_n, greet_ens, 0)
    for copy in loads:
        copy.wait()
    pl.semaphore_wait(barrier, dom_n - 1 + ens_n - 1)

    down = lax.rem(d + 1, dom_n)
    up = lax.rem(d + dom_n - 1, dom_n)
    halos = []
    for way, (src_row, dst_row, peer) in enumerate(
        ((rows_dev - HALO, 0, down), (0, HALO + rows_dev, up))
    ):
        halos.append(
            pltpu.make_async_remote_copy(
                src_ref=ext.at[:, pl.ds(HALO + src_row, HALO), :],
                dst_ref=ext.at[:, pl.ds(dst_row, HALO), :],
                send_sem=h_send.at[way * 4],
                recv_sem=h_recv.at[way * 4],
                device_id=(e, peer),
                device_id_type=MESH,
            )
        )
        for i in range(3):
            halos.append(
                pltpu.make_async_remote_copy(
                    src_ref=cext.at[i, pl.ds(HALO + src_row, HALO), :],
                    dst_ref=cext.at[i, pl.ds(dst_row, HALO), :],
                    send_sem=h_send.at[way * 4 + 1 + i],
                    recv_sem=h_recv.at[way * 4 + 1 + i],
                    device_id=(e, peer),
                    device_id_type=MESH,
                )
            )
    for copy in halos:
        copy.start()

    offs = jnp.zeros((1, nob), jnp.int32)
    for b in range(nb):
        offs = offs + off[pl.ds(b, 1), :] * (own[b] == d).astype(jnp.int32)
    lane_of = lax.rem(offs, cols)
    row_of = lax.div(offs, cols)
    lane_hot[...] = (
        lax.broadcasted_iota(jnp.int32, (cols, nob), 0) == lane_of
    ).astype(jnp.float32).astype(jnp.bfloat16)
    row_hot[...] = (
        lax.broadcasted_iota(jnp.int32, (rows_dev, nob), 0) == row_of
    ).astype(jnp.float32)

    def turn(first, count):
        def one(m, carry):
            cells[pl.ds(first * mem_loc + m, count, stride=mem_loc), :] = ext[m, pl.ds(first, count), :]
            return carry

        lax.fori_loop(0, mem_loc, one, 0, unroll=4)

    turn(HALO, rows_dev)
    for copy in halos:
        copy.wait_recv()
    turn(0, HALO)
    turn(HALO + rows_dev, HALO)
    rc, cc, df = cext[0], cext[1], cext[2]
    weight[0] = 1.0 - rc - cc - 4.0 * df
    weight[1] = rc + df
    weight[2] = cc + df
    weight[3] = df

    def at_row(r):
        return pl.ds(pl.multiple_of(r * mem_loc, mem_loc), mem_loc)

    def coef(i, r):
        return jnp.broadcast_to(weight[i, pl.ds(r, 1), :], (mem_loc, cols))

    for step in range(FSTEPS):
        first = HALO - (FSTEPS - 1 - step)
        last = HALO + rows_dev + (FSTEPS - 1 - step)

        src, dst = (cells, other) if step % 2 == 0 else (other, cells)

        def one(r, carry, step=step, src=src, dst=dst):
            above, here = carry
            below = src[at_row(r + 1), :]
            left = pltpu.roll(here, 1, 1)
            right = pltpu.roll(here, cols - 1, 1)
            fresh = (
                coef(0, r) * here
                + coef(1, r) * above
                + coef(2, r) * left
                + coef(3, r) * (below + right)
            )
            if step < FSTEPS - 1:
                dst[at_row(r), :] = fresh
            else:
                full[e, at_row(r - HALO), :] = fresh
            return here, below

        lax.fori_loop(
            first, last, one, (src[at_row(first - 1), :], src[at_row(first), :]), unroll=4
        )

    half = rows_dev * mem_loc // 2

    def g_copy(way, part, step, arriving):
        shift = step + 1 if arriving else step
        block = lax.rem(e - shift + ens_n, ens_n) if way == 0 else lax.rem(e + shift, ens_n)
        peer = lax.rem(e + 1, ens_n) if way == 0 else lax.rem(e + ens_n - 1, ens_n)
        where = full.at[block, pl.ds(pl.multiple_of(part * half, half), half), :]
        slot = (way * 2 + part) * 4 + step
        return pltpu.make_async_remote_copy(
            src_ref=where,
            dst_ref=where,
            send_sem=g_send.at[slot],
            recv_sem=g_recv.at[slot],
            device_id=(peer, d),
            device_id_type=MESH,
        )

    def g_start(part, step):
        for way in (0, 1):
            g_copy(way, part, step, False).start()

    def g_wait(part, step):
        for way in (0, 1):
            g_copy(way, part, step, True).wait_recv()

    g_start(0, 0)

    rows_once = 4

    def pick(i, acc):
        block = pl.ds(pl.multiple_of(i * rows_once * mem_loc, rows_once * mem_loc), rows_once * mem_loc)
        hi, lo = split2(full[e, block, :])
        hot = lane_hot[...]
        picked = bdot(hi, hot) + bdot(lo, hot)
        for j in range(rows_once):
            acc = acc + picked[j * mem_loc : (j + 1) * mem_loc] * row_hot[
                pl.ds(i * rows_once + j, 1), :
            ]
        return acc

    hx[...] = lax.fori_loop(
        0, rows_dev // rows_once, pick, jnp.zeros((mem_loc, nob), jnp.float32), unroll=2
    )

    def a_copy(src, dst, peer):
        return pltpu.make_async_remote_copy(
            src_ref=hx.at[pl.ds(src, 1), :],
            dst_ref=a_in.at[dst],
            send_sem=a_send.at[peer],
            recv_sem=a_recv.at[dst],
            device_id=(e, peer),
            device_id_type=MESH,
        )

    def a_start(i, carry):
        peer = lax.rem(d + i, dom_n)
        a_copy(peer, d, peer).start()
        return carry

    def a_wait(i, carry):
        peer = lax.rem(d + i, dom_n)
        a_copy(peer, peer, peer).wait_recv()
        return carry

    lax.fori_loop(1, dom_n, a_start, 0)
    a_in[d] = hx[pl.ds(d, 1), :]

    lax.fori_loop(1, dom_n, a_wait, 0)

    for b in range(nb):
        row = a_in[own[b]]
        for p in range(parts):
            piece = row[:, p * cols : (p + 1) * cols]
            b_out[b, p] = piece
            c_src[b, p, pl.ds(e, 1), :] = piece

    def b_copy(slot, peer):
        return pltpu.make_async_remote_copy(
            src_ref=b_out,
            dst_ref=c_src.at[:, :, pl.ds(slot, 1), :],
            send_sem=b_send.at[peer],
            recv_sem=b_recv.at[slot],
            device_id=(peer, d),
            device_id_type=MESH,
        )

    def b_start(i, carry):
        peer = lax.rem(e + i, ens_n)
        b_copy(e, peer).start()
        return carry

    def b_wait(i, carry):
        peer = lax.rem(e + i, ens_n)
        b_copy(peer, peer).wait_recv()
        return carry

    lax.fori_loop(1, ens_n, b_start, 0)
    g_start(1, 0)
    lax.fori_loop(1, ens_n, b_wait, 0)

    spans = ((0, 1), (1, nb - 1))

    def c_copy(part, slot, peer):
        first, count = spans[part]
        return pltpu.make_async_remote_copy(
            src_ref=c_src.at[pl.ds(first, count)],
            dst_ref=arrived.at[
                pl.ds(first, count), :, pl.ds(pl.multiple_of(slot * ens_n, ens_n), ens_n), :
            ],
            send_sem=c_send.at[part * dom_n + peer],
            recv_sem=c_recv.at[part * dom_n + slot],
            device_id=(e, peer),
            device_id_type=MESH,
        )

    def c_start(part):
        def one(i, carry):
            peer = lax.rem(d + i, dom_n)
            c_copy(part, d, peer).start()
            return carry

        lax.fori_loop(1, dom_n, one, 0)

    def c_wait(part):
        def one(i, carry):
            peer = lax.rem(d + i, dom_n)
            c_copy(part, peer, peer).wait_recv()
            return carry

        lax.fori_loop(1, dom_n, one, 0)

    c_start(0)
    c_start(1)
    g_wait(0, 0)
    g_start(0, 1)
    arrived[:, :, pl.ds(pl.multiple_of(d * ens_n, ens_n), ens_n), :] = c_src[...]
    c_wait(0)
    g_wait(1, 0)
    g_start(1, 1)

    def in_order(b):
        columns = [
            jnp.concatenate(
                [arrived.at[b, p][pl.ds(k, mem_loc, stride=ens_n), :] for k in range(ens_n)], axis=0
            )
            for p in range(parts)
        ]
        return jnp.concatenate(columns, axis=1)

    eye = (
        lax.broadcasted_iota(jnp.int32, (members, members), 0)
        == lax.broadcasted_iota(jnp.int32, (members, members), 1)
    ).astype(jnp.float32)
    scale = 1.0 / (members - 1.0)
    low = members + PAD

    def analyse(observed, b):
        ybar = jnp.sum(observed, axis=0, keepdims=True) * (1.0 / members)
        rs = 1.0 / jnp.sqrt(var[pl.ds(b, 1), :])
        anom = (observed - ybar) * rs
        innov = (obs[pl.ds(b, 1), :] - ybar) * rs
        left = jnp.concatenate([anom, jnp.broadcast_to(innov, (PAD, nob))], axis=0)
        both = dot_nt(left, anom) * scale
        gram = both[:members]
        z = both[members:]
        size = 1.001 * jnp.sqrt(jnp.sum(gram * gram, keepdims=True))
        alpha = 2.0 / (2.0 + size)
        r = size / (2.0 + size)
        k_mat = eye + gram
        gram_s[...] = k_mat
        err = eye - alpha * k_mat
        a = 2.0 / (2.0 - r * r)
        prod = dot(jnp.concatenate([z, err], axis=0), err)
        first = a * alpha
        pair[:members] = first * (eye + err)
        pair[members:low] = first * (z + prod[:PAD])
        pair[low:] = a * prod[PAD:] - (a - 1.0) * eye
        r = a - 1.0

        def advance(r, held, prod):
            a = 2.0 / (2.0 - r * r)
            pair[:low] = a * (held[:low] + prod[:low])
            pair[low:] = a * prod[low:] - (a - 1.0) * eye
            return a - 1.0

        held = pair[...]
        r = advance(r, held, dot(held, held[low:]))

        def step(i, r):
            held = pair[...]
            hi, lo = split2(held)
            return advance(r, held, dot3((hi, lo), (hi[low:], lo[low:])))

        r = lax.fori_loop(0, 3, step, r)
        serve(b, 0)
        r = lax.fori_loop(3, 6, step, r)
        a = 2.0 / (2.0 - r * r)
        x = pair[:low]
        x = a * (x + dot3(split2(x), split2(pair[low:])))
        rest = eye - dot(gram_s[...], x[:members])
        x = x + dot3(split2(x), split2(rest))
        want = (lax.broadcasted_iota(jnp.int32, (low, 1), 0) < members).astype(jnp.float32)
        return x + (want - jnp.sum(x, axis=1, keepdims=True)) * (1.0 / members)

    def update(x, columns):
        prod = dot3(x, split2(columns))
        return 0.5 * (columns + prod[:members]) + prod[members : members + 1]

    prior[0] = in_order(0)

    def serve(b, place):
        @pl.when(b < 2)
        def _():
            step = 2 + b
            g_wait(place, step - 1)
            for way in (0, 1):

                @pl.when((b < 1) | (place == way))
                def _():
                    g_copy(way, place, step, False).start()

    rows = pl.ds(pl.multiple_of(e * mem_loc, mem_loc), mem_loc)

    def batch(b, carry):
        x = analyse(prior[b], b)
        serve(b, 1)
        x2 = split2(x)

        @pl.when(b == 0)
        def _():
            total[...] = 0.5 * (eye + x[:members]) + x[members : members + 1]
            c_wait(1)
            for later in range(1, nb):
                prior[later] = in_order(later)

        def later_one(later, carry):
            prior[later] = update(x2, prior[later])
            return carry

        lax.fori_loop(b + 1, nb, later_one, 0)

        @pl.when((b > 0) & (b < nb - 1))
        def _():
            total[...] = update(x2, total[...])

        @pl.when(b == nb - 1)
        def _():
            pair[:low] = x
            thin = jnp.concatenate([pair[rows, :], x[members:]], axis=0)
            prod = dot3(split2(thin), split2(total[...]))
            t_own[...] = (
                0.5 * (total[rows, :] + prod[:mem_loc]) + prod[mem_loc : mem_loc + 1]
            )

        return carry

    lax.fori_loop(0, nb, batch, 0)
    g_copy(0, 0, 3, True).wait_recv()
    g_copy(1, 1, 3, True).wait_recv()

    hi, lo = split2(t_own[...])
    both = jnp.concatenate([hi, lo], axis=0)

    def apply(i, carry):
        pieces = [
            jnp.concatenate(
                [
                    full[k, pl.ds(pl.multiple_of((2 * i + j) * mem_loc, mem_loc), mem_loc), :]
                    for k in range(ens_n)
                ],
                axis=0,
            )
            for j in range(2)
        ]
        x_hi, x_lo = split2(jnp.concatenate(pieces, axis=1))
        one = bdot(both, x_hi)
        res = one[:mem_loc] + one[mem_loc:] + bdot(hi, x_lo)
        out[pl.ds(2 * i, mem_loc, stride=rows_dev), :] = res[:, :cols]
        out[pl.ds(2 * i + 1, mem_loc, stride=rows_dev), :] = res[:, cols:]
        return carry

    lax.fori_loop(0, rows_dev // 2, apply, 0, unroll=2)

    for copy in halos:
        copy.wait_send()
    for way in (0, 1):
        for part in (0, 1):
            for step in range(4 if way == part else 3):
                g_copy(way, part, step, False).wait_send()

    def sent_dom(i, carry):
        peer = lax.rem(d + i, dom_n)
        a_copy(peer, d, peer).wait_send()
        c_copy(0, d, peer).wait_send()
        c_copy(1, d, peer).wait_send()
        return carry

    def sent_ens(i, carry):
        b_copy(e, lax.rem(e + i, ens_n)).wait_send()
        return carry

    lax.fori_loop(1, dom_n, sent_dom, 0)
    lax.fori_loop(1, ens_n, sent_ens, 0)


def on_device(mesh_shape, state, row_c, col_c, diff, obs, var, off, owners):
    ens_n, dom_n = mesh_shape
    mem_loc, rows_dev, cols = state.shape
    members = mem_loc * ens_n
    nb, nob = obs.shape
    high = rows_dev + 2 * HALO
    f32 = jnp.float32
    sem = pltpu.SemaphoreType.DMA
    assert ens_n == 8 and nb == 4
    hbm = pl.BlockSpec(memory_space=pl.ANY)
    vmem = pl.BlockSpec(memory_space=pltpu.VMEM)
    result = pl.pallas_call(
        kernel,
        out_shape=jax.ShapeDtypeStruct((mem_loc * rows_dev, cols), f32),
        in_specs=[hbm] * 8,
        out_specs=vmem,
        scratch_shapes=[
            pltpu.VMEM((mem_loc, high, cols), f32),
            pltpu.VMEM((3, high, cols), f32),
            pltpu.VMEM((high * mem_loc, cols), f32),
            pltpu.VMEM((high * mem_loc, cols), f32),
            pltpu.VMEM((4, high, cols), f32),
            pltpu.VMEM((ens_n, rows_dev * mem_loc, cols), f32),
            pltpu.VMEM((nb, nob), f32),
            pltpu.VMEM((nb, nob), f32),
            pltpu.VMEM((nb, nob), jnp.int32),
            pltpu.SMEM((nb,), jnp.int32),
            pltpu.VMEM((cols, nob), jnp.bfloat16),
            pltpu.VMEM((rows_dev, nob), f32),
            pltpu.VMEM((mem_loc, nob), f32),
            pltpu.VMEM((dom_n, 1, nob), f32),
            pltpu.VMEM((nb, nob // cols, 1, cols), f32),
            pltpu.VMEM((nb, nob // cols, ens_n, cols), f32),
            pltpu.VMEM((nb, nob // cols, members, cols), f32),
            pltpu.VMEM((nb, members, nob), f32),
            pltpu.VMEM((2 * members + PAD, members), f32),
            pltpu.VMEM((members, members), f32),
            pltpu.VMEM((members, members), f32),
            pltpu.VMEM((mem_loc, members), f32),
            sem((8,)),
            sem((8,)),
            sem((8,)),
            sem((dom_n,)),
            sem((dom_n,)),
            sem((ens_n,)),
            sem((ens_n,)),
            sem((2 * dom_n,)),
            sem((2 * dom_n,)),
            sem((16,)),
            sem((16,)),
        ],
        compiler_params=pltpu.CompilerParams(
            collective_id=0, has_side_effects=True, vmem_limit_bytes=60 * 1024 * 1024
        ),
    )(state, row_c, col_c, diff, obs, var, off, owners)
    return result.reshape(mem_loc, rows_dev, cols)


def solution(mesh):
    sizes = (mesh.shape["ens"], mesh.shape["dom"])
    return jax.shard_map(
        functools.partial(on_device, sizes),
        mesh=mesh,
        in_specs=(
            P("ens", "dom", None),
            P("dom", None),
            P("dom", None),
            P("dom", None),
            P(),
            P(),
            P(),
            P(),
        ),
        out_specs=P("ens", "dom", None),
        check_vma=False,
    )
```

```python
import functools

import jax
import jax.numpy as jnp
from jax import lax
from jax.experimental import pallas as pl
from jax.experimental.pallas import tpu as pltpu
from jax.sharding import PartitionSpec as P

MESH = pl.DeviceIdType.MESH
FSTEPS = 4
HALO = 8
PAD = 8


def split2(x):
    hi = x.astype(jnp.bfloat16)
    lo = (x - hi.astype(jnp.float32)).astype(jnp.bfloat16)
    return hi, lo


def dot6(a, b, transposed=False):
    a_hi, a_mid, a_lo = a
    b_hi, b_mid, b_lo = b
    axis = 1 if transposed else 0
    left = jnp.concatenate([a_hi, a_mid, a_hi, a_mid, a_lo, a_hi], axis=1)
    right = jnp.concatenate([b_hi, b_hi, b_mid, b_mid, b_hi, b_lo], axis=axis)
    return lax.dot_general(
        left, right, (((1,), (axis,)), ((), ())), preferred_element_type=jnp.float32
    )


def split3(x):
    hi = x.astype(jnp.bfloat16)
    rest = x - hi.astype(jnp.float32)
    mid = rest.astype(jnp.bfloat16)
    lo = (rest - mid.astype(jnp.float32)).astype(jnp.bfloat16)
    return hi, mid, lo


def bdot(a, b):
    return jnp.dot(a, b, preferred_element_type=jnp.float32)


def dot3(a, b):
    a_hi, a_lo = a
    b_hi, b_lo = b
    return bdot(
        jnp.concatenate([a_hi, a_lo, a_hi], axis=1), jnp.concatenate([b_hi, b_hi, b_lo], axis=0)
    )


def kernel(
    state, row_c, col_c, diff, obs_in, var_in, off_in, own_in, out,
    ext, cext, cells, other, weight, full, obs, var, off, own, lane_hot, row_hot, hx, a_in, b_out, c_src,
    arrived, prior, pair, gram_s, total, t_own,
    load_sem, h_send, h_recv, a_send, a_recv, b_send, b_recv, c_send, c_recv, g_send, g_recv,
):
    ens_n = lax.axis_size("ens")
    dom_n = lax.axis_size("dom")
    e = lax.axis_index("ens")
    d = lax.axis_index("dom")
    mem_loc, rows_dev, cols = state.shape
    members = mem_loc * ens_n
    nb, nob = obs.shape
    parts = nob // cols
    high = rows_dev + 2 * HALO

    inner = pl.ds(HALO, rows_dev)
    moves = [(state, ext.at[:, inner, :])]
    moves += [(coef, cext.at[i, inner, :]) for i, coef in enumerate((row_c, col_c, diff))]
    moves += [(obs_in, obs), (var_in, var), (off_in, off), (own_in, own)]
    loads = [pltpu.make_async_copy(src, dst, load_sem.at[i]) for i, (src, dst) in enumerate(moves)]
    for copy in loads:
        copy.start()

    barrier = pltpu.get_barrier_semaphore()

    def greet_dom(i, carry):
        pl.semaphore_signal(
            barrier, inc=1, device_id=(e, lax.rem(d + i, dom_n)), device_id_type=MESH
        )
        return carry

    def greet_ens(i, carry):
        pl.semaphore_signal(
            barrier, inc=1, device_id=(lax.rem(e + i, ens_n), d), device_id_type=MESH
        )
        return carry

    lax.fori_loop(1, dom_n, greet_dom, 0)
    lax.fori_loop(1, ens_n, greet_ens, 0)
    for copy in loads:
        copy.wait()
    pl.semaphore_wait(barrier, dom_n - 1 + ens_n - 1)

    down = lax.rem(d + 1, dom_n)
    up = lax.rem(d + dom_n - 1, dom_n)
    halos = []
    for way, (src_row, dst_row, peer) in enumerate(
        ((rows_dev - HALO, 0, down), (0, HALO + rows_dev, up))
    ):
        halos.append(
            pltpu.make_async_remote_copy(
                src_ref=ext.at[:, pl.ds(HALO + src_row, HALO), :],
                dst_ref=ext.at[:, pl.ds(dst_row, HALO), :],
                send_sem=h_send.at[way * 4],
                recv_sem=h_recv.at[way * 4],
                device_id=(e, peer),
                device_id_type=MESH,
            )
        )
        for i in range(3):
            halos.append(
                pltpu.make_async_remote_copy(
                    src_ref=cext.at[i, pl.ds(HALO + src_row, HALO), :],
                    dst_ref=cext.at[i, pl.ds(dst_row, HALO), :],
                    send_sem=h_send.at[way * 4 + 1 + i],
                    recv_sem=h_recv.at[way * 4 + 1 + i],
                    device_id=(e, peer),
                    device_id_type=MESH,
                )
            )
    for copy in halos:
        copy.start()

    offs = jnp.zeros((1, nob), jnp.int32)
    for b in range(nb):
        offs = offs + off[pl.ds(b, 1), :] * (own[b] == d).astype(jnp.int32)
    lane_of = lax.rem(offs, cols)
    row_of = lax.div(offs, cols)
    lane_hot[...] = (
        lax.broadcasted_iota(jnp.int32, (cols, nob), 0) == lane_of
    ).astype(jnp.float32).astype(jnp.bfloat16)
    row_hot[...] = (
        lax.broadcasted_iota(jnp.int32, (rows_dev, nob), 0) == row_of
    ).astype(jnp.float32)

    def turn(first, count):
        def one(m, carry):
            cells[pl.ds(first * mem_loc + m, count, stride=mem_loc), :] = ext[m, pl.ds(first, count), :]
            return carry

        lax.fori_loop(0, mem_loc, one, 0, unroll=4)

    turn(HALO, rows_dev)
    for copy in halos:
        copy.wait_recv()
    turn(0, HALO)
    turn(HALO + rows_dev, HALO)
    rc, cc, df = cext[0], cext[1], cext[2]
    weight[0] = 1.0 - rc - cc - 4.0 * df
    weight[1] = rc + df
    weight[2] = cc + df
    weight[3] = df

    def at_row(r):
        return pl.ds(pl.multiple_of(r * mem_loc, mem_loc), mem_loc)

    def coef(i, r):
        return jnp.broadcast_to(weight[i, pl.ds(r, 1), :], (mem_loc, cols))

    for step in range(FSTEPS):
        first = HALO - (FSTEPS - 1 - step)
        last = HALO + rows_dev + (FSTEPS - 1 - step)

        src, dst = (cells, other) if step % 2 == 0 else (other, cells)

        def one(r, carry, step=step, src=src, dst=dst):
            above, here = carry
            below = src[at_row(r + 1), :]
            left = pltpu.roll(here, 1, 1)
            right = pltpu.roll(here, cols - 1, 1)
            fresh = (
                coef(0, r) * here
                + coef(1, r) * above
                + coef(2, r) * left
                + coef(3, r) * (below + right)
            )
            if step < FSTEPS - 1:
                dst[at_row(r), :] = fresh
            else:
                full[e, at_row(r - HALO), :] = fresh
            return here, below

        lax.fori_loop(
            first,
            last,
            one,
            (src[at_row(first - 1), :], src[at_row(first), :]),
            unroll=(last - first) // 2,
        )

    half = rows_dev * mem_loc // 2

    def g_copy(way, part, step, arriving):
        shift = step + 1 if arriving else step
        block = lax.rem(e - shift + ens_n, ens_n) if way == 0 else lax.rem(e + shift, ens_n)
        peer = lax.rem(e + 1, ens_n) if way == 0 else lax.rem(e + ens_n - 1, ens_n)
        where = full.at[block, pl.ds(pl.multiple_of(part * half, half), half), :]
        slot = (way * 2 + part) * 4 + step
        return pltpu.make_async_remote_copy(
            src_ref=where,
            dst_ref=where,
            send_sem=g_send.at[slot],
            recv_sem=g_recv.at[slot],
            device_id=(peer, d),
            device_id_type=MESH,
        )

    def g_start(part, step):
        for way in (0, 1):
            g_copy(way, part, step, False).start()

    def g_wait(part, step):
        for way in (0, 1):
            g_copy(way, part, step, True).wait_recv()

    g_start(0, 0)

    rows_once = 4

    def pick(i, acc):
        block = pl.ds(pl.multiple_of(i * rows_once * mem_loc, rows_once * mem_loc), rows_once * mem_loc)
        hi, lo = split2(full[e, block, :])
        hot = lane_hot[...]
        picked = bdot(hi, hot) + bdot(lo, hot)
        for j in range(rows_once):
            acc = acc + picked[j * mem_loc : (j + 1) * mem_loc] * row_hot[
                pl.ds(i * rows_once + j, 1), :
            ]
        return acc

    hx[...] = lax.fori_loop(
        0, rows_dev // rows_once, pick, jnp.zeros((mem_loc, nob), jnp.float32), unroll=2
    )

    def a_copy(src, dst, peer):
        return pltpu.make_async_remote_copy(
            src_ref=hx.at[pl.ds(src, 1), :],
            dst_ref=a_in.at[dst],
            send_sem=a_send.at[peer],
            recv_sem=a_recv.at[dst],
            device_id=(e, peer),
            device_id_type=MESH,
        )

    def a_start(i, carry):
        peer = lax.rem(d + i, dom_n)
        a_copy(peer, d, peer).start()
        return carry

    def a_wait(i, carry):
        peer = lax.rem(d + i, dom_n)
        a_copy(peer, peer, peer).wait_recv()
        return carry

    lax.fori_loop(1, dom_n, a_start, 0)
    a_in[d] = hx[pl.ds(d, 1), :]

    lax.fori_loop(1, dom_n, a_wait, 0)

    for b in range(nb):
        row = a_in[own[b]]
        for p in range(parts):
            piece = row[:, p * cols : (p + 1) * cols]
            b_out[b, p] = piece
            c_src[b, p, pl.ds(e, 1), :] = piece

    def b_copy(slot, peer):
        return pltpu.make_async_remote_copy(
            src_ref=b_out,
            dst_ref=c_src.at[:, :, pl.ds(slot, 1), :],
            send_sem=b_send.at[peer],
            recv_sem=b_recv.at[slot],
            device_id=(peer, d),
            device_id_type=MESH,
        )

    def b_start(i, carry):
        peer = lax.rem(e + i, ens_n)
        b_copy(e, peer).start()
        return carry

    def b_wait(i, carry):
        peer = lax.rem(e + i, ens_n)
        b_copy(peer, peer).wait_recv()
        return carry

    lax.fori_loop(1, ens_n, b_start, 0)
    g_start(1, 0)
    lax.fori_loop(1, ens_n, b_wait, 0)

    spans = ((0, 1), (1, nb - 1))

    def c_copy(part, slot, peer):
        first, count = spans[part]
        return pltpu.make_async_remote_copy(
            src_ref=c_src.at[pl.ds(first, count)],
            dst_ref=arrived.at[
                pl.ds(first, count), :, pl.ds(pl.multiple_of(slot * ens_n, ens_n), ens_n), :
            ],
            send_sem=c_send.at[part * dom_n + peer],
            recv_sem=c_recv.at[part * dom_n + slot],
            device_id=(e, peer),
            device_id_type=MESH,
        )

    def c_start(part):
        def one(i, carry):
            peer = lax.rem(d + i, dom_n)
            c_copy(part, d, peer).start()
            return carry

        lax.fori_loop(1, dom_n, one, 0)

    def c_wait(part):
        def one(i, carry):
            peer = lax.rem(d + i, dom_n)
            c_copy(part, peer, peer).wait_recv()
            return carry

        lax.fori_loop(1, dom_n, one, 0)

    c_start(0)
    c_start(1)
    g_wait(0, 0)
    g_start(0, 1)
    arrived[:, :, pl.ds(pl.multiple_of(d * ens_n, ens_n), ens_n), :] = c_src[...]
    c_wait(0)
    g_wait(1, 0)
    g_start(1, 1)

    def in_order(b):
        columns = [
            jnp.concatenate(
                [arrived.at[b, p][pl.ds(k, mem_loc, stride=ens_n), :] for k in range(ens_n)], axis=0
            )
            for p in range(parts)
        ]
        return jnp.concatenate(columns, axis=1)

    eye = (
        lax.broadcasted_iota(jnp.int32, (members, members), 0)
        == lax.broadcasted_iota(jnp.int32, (members, members), 1)
    ).astype(jnp.float32)
    scale = 1.0 / (members - 1.0)
    low = members + PAD

    def analyse(observed, b):
        ybar = jnp.sum(observed, axis=0, keepdims=True) * (1.0 / members)
        rs = 1.0 / jnp.sqrt(var[pl.ds(b, 1), :])
        anom = (observed - ybar) * rs
        innov = (obs[pl.ds(b, 1), :] - ybar) * rs
        left = split3(jnp.concatenate([anom, jnp.broadcast_to(innov, (PAD, nob))], axis=0))
        both = dot6(left, [piece[:members] for piece in left], True) * scale
        gram = both[:members]
        z = both[members:]
        size = 1.001 * jnp.sqrt(jnp.sum(gram * gram, keepdims=True))
        alpha = 2.0 / (2.0 + size)
        r = size / (2.0 + size)
        k_mat = eye + gram
        gram_s[...] = k_mat
        err = eye - alpha * k_mat
        a = 2.0 / (2.0 - r * r)
        first = a * alpha
        pair[:members] = first * (eye + err)
        hi, lo = split2(jnp.concatenate([z, err], axis=0))
        prod = dot3((hi, lo), (hi[PAD:], lo[PAD:]))
        pair[members:low] = first * (z + prod[:PAD])
        pair[low:] = a * prod[PAD:] - (a - 1.0) * eye

        def advance(r, held, prod):
            a = 2.0 / (2.0 - r * r)
            pair[:low] = a * (held[:low] + prod[:low])
            pair[low:] = a * prod[low:] - (a - 1.0) * eye
            return a - 1.0

        def step(i, r):
            held = pair[...]
            hi, lo = split2(held)
            return advance(r, held, dot3((hi, lo), (hi[low:], lo[low:])))

        r = lax.fori_loop(0, 4, step, a - 1.0)
        serve(b)
        r = lax.fori_loop(4, 7, step, r)
        a = 2.0 / (2.0 - r * r)
        x = pair[:low]
        x = a * (x + dot3(split2(x), split2(pair[low:])))
        x2 = split2(x)
        rest = eye - dot3(split2(gram_s[...]), (x2[0][:members], x2[1][:members]))
        x = x + dot3(x2, split2(rest))
        rest = eye - dot6(split3(gram_s[...]), split3(x[:members]))
        x = x + dot3(split2(x), split2(rest))
        want = (lax.broadcasted_iota(jnp.int32, (low, 1), 0) < members).astype(jnp.float32)
        return x + (want - jnp.sum(x, axis=1, keepdims=True)) * (1.0 / members)

    def update(x, columns):
        prod = dot3(x, split2(columns))
        return 0.5 * (columns + prod[:members]) + prod[members : members + 1]

    prior[0] = in_order(0)

    def serve(b):
        part = lax.rem(b, 2)
        step = 2 + lax.div(b, 2)
        g_wait(part, step - 1)
        for way in (0, 1):

            @pl.when((b < 2) | (part == way))
            def _():
                g_copy(way, part, step, False).start()

    rows = pl.ds(pl.multiple_of(e * mem_loc, mem_loc), mem_loc)

    def batch(b, carry):
        x = analyse(prior[b], b)
        x2 = split2(x)

        @pl.when(b == 0)
        def _():
            total[...] = 0.5 * (eye + x[:members]) + x[members : members + 1]
            c_wait(1)
            for later in range(1, nb):
                prior[later] = in_order(later)

        def later_one(later, carry):
            prior[later] = update(x2, prior[later])
            return carry

        lax.fori_loop(b + 1, nb, later_one, 0)

        @pl.when((b > 0) & (b < nb - 1))
        def _():
            total[...] = update(x2, total[...])

        @pl.when(b == nb - 1)
        def _():
            pair[:low] = x
            thin = jnp.concatenate([pair[rows, :], x[members:]], axis=0)
            prod = dot3(split2(thin), split2(total[...]))
            t_own[...] = (
                0.5 * (total[rows, :] + prod[:mem_loc]) + prod[mem_loc : mem_loc + 1]
            )

        return carry

    lax.fori_loop(0, nb, batch, 0)
    g_copy(0, 0, 3, True).wait_recv()

    hi, lo = split2(t_own[...])
    both = jnp.concatenate([hi, lo], axis=0)

    def apply(i, carry):
        pieces = [
            jnp.concatenate(
                [
                    full[k, pl.ds(pl.multiple_of((2 * i + j) * mem_loc, mem_loc), mem_loc), :]
                    for k in range(ens_n)
                ],
                axis=0,
            )
            for j in range(2)
        ]
        x_hi, x_lo = split2(jnp.concatenate(pieces, axis=1))
        one = bdot(both, x_hi)
        res = one[:mem_loc] + one[mem_loc:] + bdot(hi, x_lo)
        out[pl.ds(2 * i, mem_loc, stride=rows_dev), :] = res[:, :cols]
        out[pl.ds(2 * i + 1, mem_loc, stride=rows_dev), :] = res[:, cols:]
        return carry

    lax.fori_loop(0, rows_dev // 4, apply, 0, unroll=4)
    g_copy(1, 1, 3, True).wait_recv()
    lax.fori_loop(rows_dev // 4, rows_dev // 2, apply, 0, unroll=4)

    for copy in halos:
        copy.wait_send()
    for way in (0, 1):
        for part in (0, 1):
            for step in range(4 if way == part else 3):
                g_copy(way, part, step, False).wait_send()

    def sent_dom(i, carry):
        peer = lax.rem(d + i, dom_n)
        a_copy(peer, d, peer).wait_send()
        c_copy(0, d, peer).wait_send()
        c_copy(1, d, peer).wait_send()
        return carry

    def sent_ens(i, carry):
        b_copy(e, lax.rem(e + i, ens_n)).wait_send()
        return carry

    lax.fori_loop(1, dom_n, sent_dom, 0)
    lax.fori_loop(1, ens_n, sent_ens, 0)


def on_device(mesh_shape, state, row_c, col_c, diff, obs, var, off, owners):
    ens_n, dom_n = mesh_shape
    mem_loc, rows_dev, cols = state.shape
    members = mem_loc * ens_n
    nb, nob = obs.shape
    high = rows_dev + 2 * HALO
    f32 = jnp.float32
    sem = pltpu.SemaphoreType.DMA
    assert ens_n == 8 and nb == 4
    hbm = pl.BlockSpec(memory_space=pl.ANY)
    vmem = pl.BlockSpec(memory_space=pltpu.VMEM)
    result = pl.pallas_call(
        kernel,
        out_shape=jax.ShapeDtypeStruct((mem_loc * rows_dev, cols), f32),
        in_specs=[hbm] * 8,
        out_specs=vmem,
        scratch_shapes=[
            pltpu.VMEM((mem_loc, high, cols), f32),
            pltpu.VMEM((3, high, cols), f32),
            pltpu.VMEM((high * mem_loc, cols), f32),
            pltpu.VMEM((high * mem_loc, cols), f32),
            pltpu.VMEM((4, high, cols), f32),
            pltpu.VMEM((ens_n, rows_dev * mem_loc, cols), f32),
            pltpu.VMEM((nb, nob), f32),
            pltpu.VMEM((nb, nob), f32),
            pltpu.VMEM((nb, nob), jnp.int32),
            pltpu.SMEM((nb,), jnp.int32),
            pltpu.VMEM((cols, nob), jnp.bfloat16),
            pltpu.VMEM((rows_dev, nob), f32),
            pltpu.VMEM((mem_loc, nob), f32),
            pltpu.VMEM((dom_n, 1, nob), f32),
            pltpu.VMEM((nb, nob // cols, 1, cols), f32),
            pltpu.VMEM((nb, nob // cols, ens_n, cols), f32),
            pltpu.VMEM((nb, nob // cols, members, cols), f32),
            pltpu.VMEM((nb, members, nob), f32),
            pltpu.VMEM((2 * members + PAD, members), f32),
            pltpu.VMEM((members, members), f32),
            pltpu.VMEM((members, members), f32),
            pltpu.VMEM((mem_loc, members), f32),
            sem((8,)),
            sem((8,)),
            sem((8,)),
            sem((dom_n,)),
            sem((dom_n,)),
            sem((ens_n,)),
            sem((ens_n,)),
            sem((2 * dom_n,)),
            sem((2 * dom_n,)),
            sem((16,)),
            sem((16,)),
        ],
        compiler_params=pltpu.CompilerParams(
            collective_id=0, has_side_effects=True, vmem_limit_bytes=60 * 1024 * 1024
        ),
    )(state, row_c, col_c, diff, obs, var, off, owners)
    return result.reshape(mem_loc, rows_dev, cols)


def solution(mesh):
    sizes = (mesh.shape["ens"], mesh.shape["dom"])
    return jax.shard_map(
        functools.partial(on_device, sizes),
        mesh=mesh,
        in_specs=(
            P("ens", "dom", None),
            P("dom", None),
            P("dom", None),
            P("dom", None),
            P(),
            P(),
            P(),
            P(),
        ),
        out_specs=P("ens", "dom", None),
        check_vma=False,
    )
```

```python
import functools

import jax
import jax.numpy as jnp
from jax import lax
from jax.experimental import pallas as pl
from jax.experimental.pallas import tpu as pltpu
from jax.sharding import PartitionSpec as P

MESH = pl.DeviceIdType.MESH
FSTEPS = 4
HALO = 8
PAD = 8


def split2(x):
    hi = x.astype(jnp.bfloat16)
    lo = (x - hi.astype(jnp.float32)).astype(jnp.bfloat16)
    return hi, lo


def dot6(a, b, transposed=False):
    a_hi, a_mid, a_lo = a
    b_hi, b_mid, b_lo = b
    axis = 1 if transposed else 0
    left = jnp.concatenate([a_hi, a_mid, a_hi, a_mid, a_lo, a_hi], axis=1)
    right = jnp.concatenate([b_hi, b_hi, b_mid, b_mid, b_hi, b_lo], axis=axis)
    return lax.dot_general(
        left, right, (((1,), (axis,)), ((), ())), preferred_element_type=jnp.float32
    )


def split3(x):
    hi = x.astype(jnp.bfloat16)
    rest = x - hi.astype(jnp.float32)
    mid = rest.astype(jnp.bfloat16)
    lo = (rest - mid.astype(jnp.float32)).astype(jnp.bfloat16)
    return hi, mid, lo


def bdot(a, b):
    return jnp.dot(a, b, preferred_element_type=jnp.float32)


def dot3(a, b):
    a_hi, a_lo = a
    b_hi, b_lo = b
    return bdot(
        jnp.concatenate([a_hi, a_lo, a_hi], axis=1), jnp.concatenate([b_hi, b_hi, b_lo], axis=0)
    )


def kernel(
    state, row_c, col_c, diff, obs_in, var_in, off_in, own_in, out,
    ext, cext, cells, other, weight, full, obs, var, off, own, lane_hot, row_hot, hx, a_in, b_out, c_src,
    arrived, prior, pair, gram_s, total, t_own,
    load_sem, h_send, h_recv, a_send, a_recv, b_send, b_recv, c_send, c_recv, g_send, g_recv,
):
    ens_n = lax.axis_size("ens")
    dom_n = lax.axis_size("dom")
    e = lax.axis_index("ens")
    d = lax.axis_index("dom")
    mem_loc, rows_dev, cols = state.shape
    members = mem_loc * ens_n
    nb, nob = obs.shape
    parts = nob // cols
    high = rows_dev + 2 * HALO

    inner = pl.ds(HALO, rows_dev)
    moves = [(state, ext.at[:, inner, :])]
    moves += [(coef, cext.at[i, inner, :]) for i, coef in enumerate((row_c, col_c, diff))]
    moves += [(obs_in, obs), (var_in, var), (off_in, off), (own_in, own)]
    loads = [pltpu.make_async_copy(src, dst, load_sem.at[i]) for i, (src, dst) in enumerate(moves)]
    for copy in loads:
        copy.start()

    barrier = pltpu.get_barrier_semaphore()

    def greet_dom(i, carry):
        pl.semaphore_signal(
            barrier, inc=1, device_id=(e, lax.rem(d + i, dom_n)), device_id_type=MESH
        )
        return carry

    def greet_ens(i, carry):
        pl.semaphore_signal(
            barrier, inc=1, device_id=(lax.rem(e + i, ens_n), d), device_id_type=MESH
        )
        return carry

    lax.fori_loop(1, dom_n, greet_dom, 0)
    lax.fori_loop(1, ens_n, greet_ens, 0)
    for copy in loads:
        copy.wait()
    pl.semaphore_wait(barrier, dom_n - 1 + ens_n - 1)

    down = lax.rem(d + 1, dom_n)
    up = lax.rem(d + dom_n - 1, dom_n)
    halos = []
    for way, (src_row, dst_row, peer) in enumerate(
        ((rows_dev - HALO, 0, down), (0, HALO + rows_dev, up))
    ):
        halos.append(
            pltpu.make_async_remote_copy(
                src_ref=ext.at[:, pl.ds(HALO + src_row, HALO), :],
                dst_ref=ext.at[:, pl.ds(dst_row, HALO), :],
                send_sem=h_send.at[way * 4],
                recv_sem=h_recv.at[way * 4],
                device_id=(e, peer),
                device_id_type=MESH,
            )
        )
        for i in range(3):
            halos.append(
                pltpu.make_async_remote_copy(
                    src_ref=cext.at[i, pl.ds(HALO + src_row, HALO), :],
                    dst_ref=cext.at[i, pl.ds(dst_row, HALO), :],
                    send_sem=h_send.at[way * 4 + 1 + i],
                    recv_sem=h_recv.at[way * 4 + 1 + i],
                    device_id=(e, peer),
                    device_id_type=MESH,
                )
            )
    for copy in halos:
        copy.start()

    offs = jnp.zeros((1, nob), jnp.int32)
    for b in range(nb):
        offs = offs + off[pl.ds(b, 1), :] * (own[b] == d).astype(jnp.int32)
    lane_of = lax.rem(offs, cols)
    row_of = lax.div(offs, cols)
    lane_hot[...] = (
        lax.broadcasted_iota(jnp.int32, (cols, nob), 0) == lane_of
    ).astype(jnp.float32).astype(jnp.bfloat16)
    row_hot[...] = (
        lax.broadcasted_iota(jnp.int32, (rows_dev, nob), 0) == row_of
    ).astype(jnp.float32)

    def turn(first, count):
        def one(m, carry):
            cells[pl.ds(first * mem_loc + m, count, stride=mem_loc), :] = ext[m, pl.ds(first, count), :]
            return carry

        lax.fori_loop(0, mem_loc, one, 0, unroll=4)

    turn(HALO, rows_dev)
    for copy in halos:
        copy.wait_recv()
    turn(0, HALO)
    turn(HALO + rows_dev, HALO)
    rc, cc, df = cext[0], cext[1], cext[2]
    weight[0] = 1.0 - rc - cc - 4.0 * df
    weight[1] = rc + df
    weight[2] = cc + df
    weight[3] = df

    def at_row(r):
        return pl.ds(pl.multiple_of(r * mem_loc, mem_loc), mem_loc)

    def coef(i, r):
        return jnp.broadcast_to(weight[i, pl.ds(r, 1), :], (mem_loc, cols))

    for step in range(FSTEPS):
        first = HALO - (FSTEPS - 1 - step)
        last = HALO + rows_dev + (FSTEPS - 1 - step)

        src, dst = (cells, other) if step % 2 == 0 else (other, cells)

        def one(r, carry, step=step, src=src, dst=dst):
            above, here = carry
            below = src[at_row(r + 1), :]
            left = pltpu.roll(here, 1, 1)
            right = pltpu.roll(here, cols - 1, 1)
            fresh = (
                coef(0, r) * here
                + coef(1, r) * above
                + coef(2, r) * left
                + coef(3, r) * (below + right)
            )
            if step < FSTEPS - 1:
                dst[at_row(r), :] = fresh
            else:
                full[e, at_row(r - HALO), :] = fresh
            return here, below

        lax.fori_loop(
            first,
            last,
            one,
            (src[at_row(first - 1), :], src[at_row(first), :]),
            unroll=(last - first) // 2,
        )

    half = rows_dev * mem_loc // 2

    def g_copy(way, part, step, arriving):
        shift = step + 1 if arriving else step
        block = lax.rem(e - shift + ens_n, ens_n) if way == 0 else lax.rem(e + shift, ens_n)
        peer = lax.rem(e + 1, ens_n) if way == 0 else lax.rem(e + ens_n - 1, ens_n)
        where = full.at[block, pl.ds(pl.multiple_of(part * half, half), half), :]
        slot = (way * 2 + part) * 4 + step
        return pltpu.make_async_remote_copy(
            src_ref=where,
            dst_ref=where,
            send_sem=g_send.at[slot],
            recv_sem=g_recv.at[slot],
            device_id=(peer, d),
            device_id_type=MESH,
        )

    def g_start(part, step):
        for way in (0, 1):
            g_copy(way, part, step, False).start()

    def g_wait(part, step):
        for way in (0, 1):
            g_copy(way, part, step, True).wait_recv()

    g_start(0, 0)

    rows_once = 4

    def pick(i, acc):
        block = pl.ds(pl.multiple_of(i * rows_once * mem_loc, rows_once * mem_loc), rows_once * mem_loc)
        hi, lo = split2(full[e, block, :])
        hot = lane_hot[...]
        picked = bdot(hi, hot) + bdot(lo, hot)
        for j in range(rows_once):
            acc = acc + picked[j * mem_loc : (j + 1) * mem_loc] * row_hot[
                pl.ds(i * rows_once + j, 1), :
            ]
        return acc

    hx[...] = lax.fori_loop(
        0, rows_dev // rows_once, pick, jnp.zeros((mem_loc, nob), jnp.float32), unroll=2
    )

    def a_copy(src, dst, peer, turn_at):
        return pltpu.make_async_remote_copy(
            src_ref=hx.at[pl.ds(src, 1), :],
            dst_ref=a_in.at[dst],
            send_sem=a_send.at[turn_at],
            recv_sem=a_recv.at[dst],
            device_id=(e, peer),
            device_id_type=MESH,
        )

    def a_start(i, carry):
        peer = lax.rem(d + i, dom_n)
        a_copy(peer, d, peer, i).start()
        return carry

    def a_wait(i, carry):
        peer = lax.rem(d + i, dom_n)
        a_copy(peer, peer, peer, i).wait_recv()
        return carry

    lax.fori_loop(1, dom_n, a_start, 0)
    a_in[d] = hx[pl.ds(d, 1), :]

    lax.fori_loop(1, dom_n, a_wait, 0)

    for b in range(nb):
        row = a_in[own[b]]
        for p in range(parts):
            piece = row[:, p * cols : (p + 1) * cols]
            b_out[b, p] = piece
            c_src[b, p, pl.ds(e, 1), :] = piece

    def b_copy(slot, peer, turn_at):
        return pltpu.make_async_remote_copy(
            src_ref=b_out,
            dst_ref=c_src.at[:, :, pl.ds(slot, 1), :],
            send_sem=b_send.at[turn_at],
            recv_sem=b_recv.at[slot],
            device_id=(peer, d),
            device_id_type=MESH,
        )

    def b_start(i, carry):
        peer = lax.rem(e + i, ens_n)
        b_copy(e, peer, i).start()
        return carry

    def b_wait(i, carry):
        peer = lax.rem(e + i, ens_n)
        b_copy(peer, peer, i).wait_recv()
        return carry

    lax.fori_loop(1, ens_n, b_start, 0)
    g_start(1, 0)
    lax.fori_loop(1, ens_n, b_wait, 0)

    spans = ((0, 1), (1, nb - 1))

    def c_copy(part, slot, peer, turn_at):
        first, count = spans[part]
        return pltpu.make_async_remote_copy(
            src_ref=c_src.at[pl.ds(first, count)],
            dst_ref=arrived.at[
                pl.ds(first, count), :, pl.ds(pl.multiple_of(slot * ens_n, ens_n), ens_n), :
            ],
            send_sem=c_send.at[part * dom_n + turn_at],
            recv_sem=c_recv.at[part * dom_n + slot],
            device_id=(e, peer),
            device_id_type=MESH,
        )

    def c_start(part):
        def one(i, carry):
            peer = lax.rem(d + i, dom_n)
            c_copy(part, d, peer, i).start()
            return carry

        lax.fori_loop(1, dom_n, one, 0)

    def c_wait(part):
        def one(i, carry):
            peer = lax.rem(d + i, dom_n)
            c_copy(part, peer, peer, i).wait_recv()
            return carry

        lax.fori_loop(1, dom_n, one, 0)

    c_start(0)
    c_start(1)
    g_wait(0, 0)
    g_start(0, 1)
    arrived[:, :, pl.ds(pl.multiple_of(d * ens_n, ens_n), ens_n), :] = c_src[...]
    for copy in halos:
        copy.wait_send()

    def sent_a(i, carry):
        a_copy(0, d, down, i).wait_send()
        return carry

    def sent_b(i, carry):
        b_copy(e, lax.rem(e + 1, ens_n), i).wait_send()
        return carry

    lax.fori_loop(1, dom_n, sent_a, 0, unroll=True)
    lax.fori_loop(1, ens_n, sent_b, 0, unroll=True)
    c_wait(0)
    g_wait(1, 0)
    g_start(1, 1)

    def in_order(b):
        columns = [
            jnp.concatenate(
                [arrived.at[b, p][pl.ds(k, mem_loc, stride=ens_n), :] for k in range(ens_n)], axis=0
            )
            for p in range(parts)
        ]
        return jnp.concatenate(columns, axis=1)

    eye = (
        lax.broadcasted_iota(jnp.int32, (members, members), 0)
        == lax.broadcasted_iota(jnp.int32, (members, members), 1)
    ).astype(jnp.float32)
    scale = 1.0 / (members - 1.0)
    low = members + PAD

    def analyse(observed, b):
        ybar = jnp.sum(observed, axis=0, keepdims=True) * (1.0 / members)
        rs = 1.0 / jnp.sqrt(var[pl.ds(b, 1), :])
        anom = (observed - ybar) * rs
        innov = (obs[pl.ds(b, 1), :] - ybar) * rs
        left = split3(jnp.concatenate([anom, jnp.broadcast_to(innov, (PAD, nob))], axis=0))
        both = dot6(left, [piece[:members] for piece in left], True) * scale
        gram = both[:members]
        z = both[members:]
        size = 1.001 * jnp.sqrt(jnp.sum(gram * gram, keepdims=True))
        alpha = 2.0 / (2.0 + size)
        r = size / (2.0 + size)
        k_mat = eye + gram
        gram_s[...] = k_mat
        err = eye - alpha * k_mat
        a = 2.0 / (2.0 - r * r)
        first = a * alpha
        pair[:members] = first * (eye + err)
        hi, lo = split2(jnp.concatenate([z, err], axis=0))
        prod = dot3((hi, lo), (hi[PAD:], lo[PAD:]))
        pair[members:low] = first * (z + prod[:PAD])
        pair[low:] = a * prod[PAD:] - (a - 1.0) * eye

        def advance(r, held, prod):
            a = 2.0 / (2.0 - r * r)
            pair[:low] = a * (held[:low] + prod[:low])
            pair[low:] = a * prod[low:] - (a - 1.0) * eye
            return a - 1.0

        def step(i, r):
            held = pair[...]
            hi, lo = split2(held)
            return advance(r, held, dot3((hi, lo), (hi[low:], lo[low:])))

        r = lax.fori_loop(0, 4, step, a - 1.0)
        serve(b)
        r = lax.fori_loop(4, 6, step, r)
        a = 2.0 / (2.0 - r * r)
        x = pair[:low]
        x = a * (x + dot3(split2(x), split2(pair[low:])))
        r = a - 1.0
        a = 2.0 / (2.0 - r * r)
        k_parts = split3(gram_s[...])
        x2 = split2(x)
        rest = eye - dot3(k_parts[:2], (x2[0][:members], x2[1][:members]))
        x = a * (x + dot3(x2, split2(rest)))
        rest = eye - dot6(k_parts, split3(x[:members]))
        x = x + dot3(split2(x), split2(rest))
        want = (lax.broadcasted_iota(jnp.int32, (low, 1), 0) < members).astype(jnp.float32)
        return x + (want - jnp.sum(x, axis=1, keepdims=True)) * (1.0 / members)

    def update(x, columns):
        prod = dot3(x, split2(columns))
        return 0.5 * (columns + prod[:members]) + prod[members : members + 1]

    prior[0] = in_order(0)

    def serve(b):
        part = lax.rem(b, 2)
        step = 2 + lax.div(b, 2)
        g_wait(part, step - 1)
        for way in (0, 1):

            @pl.when((b < 2) | (part == way))
            def _():
                g_copy(way, part, step, False).start()

    rows = pl.ds(pl.multiple_of(e * mem_loc, mem_loc), mem_loc)

    def batch(b, carry):
        x = analyse(prior[b], b)
        x2 = split2(x)

        @pl.when(b == 0)
        def _():
            total[...] = 0.5 * (eye + x[:members]) + x[members : members + 1]
            c_wait(1)
            for later in range(1, nb):
                prior[later] = in_order(later)

        def later_one(later, carry):
            prior[later] = update(x2, prior[later])
            return carry

        lax.fori_loop(b + 1, nb, later_one, 0)

        @pl.when((b > 0) & (b < nb - 1))
        def _():
            total[...] = update(x2, total[...])

        @pl.when(b == nb - 1)
        def _():
            pair[:low] = x
            thin = jnp.concatenate([pair[rows, :], x[members:]], axis=0)
            prod = dot3(split2(thin), split2(total[...]))
            t_own[...] = (
                0.5 * (total[rows, :] + prod[:mem_loc]) + prod[mem_loc : mem_loc + 1]
            )

        return carry

    lax.fori_loop(0, nb, batch, 0)
    g_copy(0, 0, 3, True).wait_recv()

    hi, lo = split2(t_own[...])
    both = jnp.concatenate([hi, lo], axis=0)

    def apply(i, carry):
        pieces = [
            jnp.concatenate(
                [
                    full[k, pl.ds(pl.multiple_of((2 * i + j) * mem_loc, mem_loc), mem_loc), :]
                    for k in range(ens_n)
                ],
                axis=0,
            )
            for j in range(2)
        ]
        x_hi, x_lo = split2(jnp.concatenate(pieces, axis=1))
        one = bdot(both, x_hi)
        res = one[:mem_loc] + one[mem_loc:] + bdot(hi, x_lo)
        out[pl.ds(2 * i, mem_loc, stride=rows_dev), :] = res[:, :cols]
        out[pl.ds(2 * i + 1, mem_loc, stride=rows_dev), :] = res[:, cols:]
        return carry

    lax.fori_loop(0, rows_dev // 4, apply, 0, unroll=4)
    g_copy(1, 1, 3, True).wait_recv()
    lax.fori_loop(rows_dev // 4, rows_dev // 2, apply, 0, unroll=4)

    for way in (0, 1):
        for part in (0, 1):
            for step in range(4 if way == part else 3):
                g_copy(way, part, step, False).wait_send()

    def sent_c(i, carry):
        c_copy(0, d, down, i).wait_send()
        c_copy(1, d, down, i).wait_send()
        return carry

    lax.fori_loop(1, dom_n, sent_c, 0, unroll=True)


def on_device(mesh_shape, state, row_c, col_c, diff, obs, var, off, owners):
    ens_n, dom_n = mesh_shape
    mem_loc, rows_dev, cols = state.shape
    members = mem_loc * ens_n
    nb, nob = obs.shape
    high = rows_dev + 2 * HALO
    f32 = jnp.float32
    sem = pltpu.SemaphoreType.DMA
    assert ens_n == 8 and nb == 4
    hbm = pl.BlockSpec(memory_space=pl.ANY)
    vmem = pl.BlockSpec(memory_space=pltpu.VMEM)
    result = pl.pallas_call(
        kernel,
        out_shape=jax.ShapeDtypeStruct((mem_loc * rows_dev, cols), f32),
        in_specs=[hbm] * 8,
        out_specs=vmem,
        scratch_shapes=[
            pltpu.VMEM((mem_loc, high, cols), f32),
            pltpu.VMEM((3, high, cols), f32),
            pltpu.VMEM((high * mem_loc, cols), f32),
            pltpu.VMEM((high * mem_loc, cols), f32),
            pltpu.VMEM((4, high, cols), f32),
            pltpu.VMEM((ens_n, rows_dev * mem_loc, cols), f32),
            pltpu.VMEM((nb, nob), f32),
            pltpu.VMEM((nb, nob), f32),
            pltpu.VMEM((nb, nob), jnp.int32),
            pltpu.SMEM((nb,), jnp.int32),
            pltpu.VMEM((cols, nob), jnp.bfloat16),
            pltpu.VMEM((rows_dev, nob), f32),
            pltpu.VMEM((mem_loc, nob), f32),
            pltpu.VMEM((dom_n, 1, nob), f32),
            pltpu.VMEM((nb, nob // cols, 1, cols), f32),
            pltpu.VMEM((nb, nob // cols, ens_n, cols), f32),
            pltpu.VMEM((nb, nob // cols, members, cols), f32),
            pltpu.VMEM((nb, members, nob), f32),
            pltpu.VMEM((2 * members + PAD, members), f32),
            pltpu.VMEM((members, members), f32),
            pltpu.VMEM((members, members), f32),
            pltpu.VMEM((mem_loc, members), f32),
            sem((8,)),
            sem((8,)),
            sem((8,)),
            sem((dom_n,)),
            sem((dom_n,)),
            sem((ens_n,)),
            sem((ens_n,)),
            sem((2 * dom_n,)),
            sem((2 * dom_n,)),
            sem((16,)),
            sem((16,)),
        ],
        compiler_params=pltpu.CompilerParams(
            collective_id=0, has_side_effects=True, vmem_limit_bytes=60 * 1024 * 1024
        ),
    )(state, row_c, col_c, diff, obs, var, off, owners)
    return result.reshape(mem_loc, rows_dev, cols)


def solution(mesh):
    sizes = (mesh.shape["ens"], mesh.shape["dom"])
    return jax.shard_map(
        functools.partial(on_device, sizes),
        mesh=mesh,
        in_specs=(
            P("ens", "dom", None),
            P("dom", None),
            P("dom", None),
            P("dom", None),
            P(),
            P(),
            P(),
            P(),
        ),
        out_specs=P("ens", "dom", None),
        check_vma=False,
    )
```

```python
import functools

import jax
import jax.numpy as jnp
from jax import lax
from jax.experimental import pallas as pl
from jax.experimental.pallas import tpu as pltpu
from jax.sharding import PartitionSpec as P

MESH = pl.DeviceIdType.MESH
FSTEPS = 4
HALO = 8
PAD = 8


def split2(x):
    hi = x.astype(jnp.bfloat16)
    lo = (x - hi.astype(jnp.float32)).astype(jnp.bfloat16)
    return hi, lo


def dot6(a, b, transposed=False):
    a_hi, a_mid, a_lo = a
    b_hi, b_mid, b_lo = b
    axis = 1 if transposed else 0
    left = jnp.concatenate([a_hi, a_mid, a_hi, a_mid, a_lo, a_hi], axis=1)
    right = jnp.concatenate([b_hi, b_hi, b_mid, b_mid, b_hi, b_lo], axis=axis)
    return lax.dot_general(
        left, right, (((1,), (axis,)), ((), ())), preferred_element_type=jnp.float32
    )


def split3(x):
    hi = x.astype(jnp.bfloat16)
    rest = x - hi.astype(jnp.float32)
    mid = rest.astype(jnp.bfloat16)
    lo = (rest - mid.astype(jnp.float32)).astype(jnp.bfloat16)
    return hi, mid, lo


def bdot(a, b):
    return jnp.dot(a, b, preferred_element_type=jnp.float32)


def dot3(a, b):
    a_hi, a_lo = a
    b_hi, b_lo = b
    return bdot(
        jnp.concatenate([a_hi, a_lo, a_hi], axis=1), jnp.concatenate([b_hi, b_hi, b_lo], axis=0)
    )


def kernel(
    state, row_c, col_c, diff, obs_in, var_in, off_in, own_in, out,
    ext, cext, cells, other, weight, full, obs, var, off, own, lane_hot, row_hot, hx, a_in, b_out, c_src,
    arrived, prior, pair, gram_s, total, t_own,
    load_sem, h_send, h_recv, a_send, a_recv, b_send, b_recv, c_send, c_recv, g_send, g_recv,
):
    ens_n = lax.axis_size("ens")
    dom_n = lax.axis_size("dom")
    e = lax.axis_index("ens")
    d = lax.axis_index("dom")
    mem_loc, rows_dev, cols = state.shape
    members = mem_loc * ens_n
    nb, nob = obs.shape
    parts = nob // cols
    high = rows_dev + 2 * HALO

    inner = pl.ds(HALO, rows_dev)
    moves = [(state, ext.at[:, inner, :])]
    moves += [(coef, cext.at[i, inner, :]) for i, coef in enumerate((row_c, col_c, diff))]
    moves += [(obs_in, obs), (var_in, var), (off_in, off), (own_in, own)]
    loads = [pltpu.make_async_copy(src, dst, load_sem.at[i]) for i, (src, dst) in enumerate(moves)]
    for copy in loads:
        copy.start()

    barrier = pltpu.get_barrier_semaphore()

    def greet_dom(i, carry):
        pl.semaphore_signal(
            barrier, inc=1, device_id=(e, lax.rem(d + i, dom_n)), device_id_type=MESH
        )
        return carry

    def greet_ens(i, carry):
        pl.semaphore_signal(
            barrier, inc=1, device_id=(lax.rem(e + i, ens_n), d), device_id_type=MESH
        )
        return carry

    lax.fori_loop(1, dom_n, greet_dom, 0)
    lax.fori_loop(1, ens_n, greet_ens, 0)
    for copy in loads:
        copy.wait()
    pl.semaphore_wait(barrier, dom_n - 1 + ens_n - 1)

    down = lax.rem(d + 1, dom_n)
    up = lax.rem(d + dom_n - 1, dom_n)
    halos = []
    for way, (src_row, dst_row, peer) in enumerate(
        ((rows_dev - HALO, 0, down), (0, HALO + rows_dev, up))
    ):
        halos.append(
            pltpu.make_async_remote_copy(
                src_ref=ext.at[:, pl.ds(HALO + src_row, HALO), :],
                dst_ref=ext.at[:, pl.ds(dst_row, HALO), :],
                send_sem=h_send.at[way * 4],
                recv_sem=h_recv.at[way * 4],
                device_id=(e, peer),
                device_id_type=MESH,
            )
        )
        for i in range(3):
            halos.append(
                pltpu.make_async_remote_copy(
                    src_ref=cext.at[i, pl.ds(HALO + src_row, HALO), :],
                    dst_ref=cext.at[i, pl.ds(dst_row, HALO), :],
                    send_sem=h_send.at[way * 4 + 1 + i],
                    recv_sem=h_recv.at[way * 4 + 1 + i],
                    device_id=(e, peer),
                    device_id_type=MESH,
                )
            )
    for copy in halos:
        copy.start()

    offs = jnp.zeros((1, nob), jnp.int32)
    for b in range(nb):
        offs = offs + off[pl.ds(b, 1), :] * (own[b] == d).astype(jnp.int32)
    lane_of = lax.rem(offs, cols)
    row_of = lax.div(offs, cols)
    lane_hot[...] = (
        lax.broadcasted_iota(jnp.int32, (cols, nob), 0) == lane_of
    ).astype(jnp.float32).astype(jnp.bfloat16)
    row_hot[...] = (
        lax.broadcasted_iota(jnp.int32, (rows_dev, nob), 0) == row_of
    ).astype(jnp.float32)

    def turn(first, count):
        def one(m, carry):
            cells[pl.ds(first * mem_loc + m, count, stride=mem_loc), :] = ext[m, pl.ds(first, count), :]
            return carry

        lax.fori_loop(0, mem_loc, one, 0, unroll=4)

    turn(HALO, rows_dev)
    for copy in halos:
        copy.wait_recv()
    turn(0, HALO)
    turn(HALO + rows_dev, HALO)
    rc, cc, df = cext[0], cext[1], cext[2]
    weight[0] = 1.0 - rc - cc - 4.0 * df
    weight[1] = rc + df
    weight[2] = cc + df
    weight[3] = df

    def at_row(r):
        return pl.ds(pl.multiple_of(r * mem_loc, mem_loc), mem_loc)

    def coef(i, r):
        return jnp.broadcast_to(weight[i, pl.ds(r, 1), :], (mem_loc, cols))

    for step in range(FSTEPS):
        first = HALO - (FSTEPS - 1 - step)
        last = HALO + rows_dev + (FSTEPS - 1 - step)

        src, dst = (cells, other) if step % 2 == 0 else (other, cells)

        def one(r, carry, step=step, src=src, dst=dst):
            above, here = carry
            below = src[at_row(r + 1), :]
            left = pltpu.roll(here, 1, 1)
            right = pltpu.roll(here, cols - 1, 1)
            fresh = (
                coef(0, r) * here
                + coef(1, r) * above
                + coef(2, r) * left
                + coef(3, r) * (below + right)
            )
            if step < FSTEPS - 1:
                dst[at_row(r), :] = fresh
            else:
                full[e, at_row(r - HALO), :] = fresh
            return here, below

        lax.fori_loop(
            first,
            last,
            one,
            (src[at_row(first - 1), :], src[at_row(first), :]),
            unroll=(last - first) // 2,
        )

    half = rows_dev * mem_loc // 2

    def g_copy(way, part, step, arriving):
        shift = step + 1 if arriving else step
        block = lax.rem(e - shift + ens_n, ens_n) if way == 0 else lax.rem(e + shift, ens_n)
        peer = lax.rem(e + 1, ens_n) if way == 0 else lax.rem(e + ens_n - 1, ens_n)
        where = full.at[block, pl.ds(pl.multiple_of(part * half, half), half), :]
        slot = (way * 2 + part) * 4 + step
        return pltpu.make_async_remote_copy(
            src_ref=where,
            dst_ref=where,
            send_sem=g_send.at[slot],
            recv_sem=g_recv.at[slot],
            device_id=(peer, d),
            device_id_type=MESH,
        )

    def g_start(part, step):
        for way in (0, 1):
            g_copy(way, part, step, False).start()

    def g_wait(part, step):
        for way in (0, 1):
            g_copy(way, part, step, True).wait_recv()

    g_start(0, 0)

    rows_once = 4

    def pick(i, acc):
        block = pl.ds(pl.multiple_of(i * rows_once * mem_loc, rows_once * mem_loc), rows_once * mem_loc)
        hi, lo = split2(full[e, block, :])
        hot = lane_hot[...]
        picked = bdot(hi, hot) + bdot(lo, hot)
        for j in range(rows_once):
            acc = acc + picked[j * mem_loc : (j + 1) * mem_loc] * row_hot[
                pl.ds(i * rows_once + j, 1), :
            ]
        return acc

    hx[...] = lax.fori_loop(
        0, rows_dev // rows_once, pick, jnp.zeros((mem_loc, nob), jnp.float32), unroll=2
    )

    def a_copy(src, dst, peer, turn_at):
        return pltpu.make_async_remote_copy(
            src_ref=hx.at[pl.ds(src, 1), :],
            dst_ref=a_in.at[dst],
            send_sem=a_send.at[turn_at],
            recv_sem=a_recv.at[dst],
            device_id=(e, peer),
            device_id_type=MESH,
        )

    def a_start(i, carry):
        peer = lax.rem(d + i, dom_n)
        a_copy(peer, d, peer, i).start()
        return carry

    def a_wait(i, carry):
        peer = lax.rem(d + i, dom_n)
        a_copy(peer, peer, peer, i).wait_recv()
        return carry

    lax.fori_loop(1, dom_n, a_start, 0, unroll=True)
    a_in[d] = hx[pl.ds(d, 1), :]

    lax.fori_loop(1, dom_n, a_wait, 0)

    for b in range(nb):
        row = a_in[own[b]]
        for p in range(parts):
            piece = row[:, p * cols : (p + 1) * cols]
            b_out[b, p] = piece
            c_src[b, p, pl.ds(e, 1), :] = piece

    def b_copy(slot, peer, turn_at):
        return pltpu.make_async_remote_copy(
            src_ref=b_out,
            dst_ref=c_src.at[:, :, pl.ds(slot, 1), :],
            send_sem=b_send.at[turn_at],
            recv_sem=b_recv.at[slot],
            device_id=(peer, d),
            device_id_type=MESH,
        )

    def b_start(i, carry):
        peer = lax.rem(e + i, ens_n)
        b_copy(e, peer, i).start()
        return carry

    def b_wait(i, carry):
        peer = lax.rem(e + i, ens_n)
        b_copy(peer, peer, i).wait_recv()
        return carry

    lax.fori_loop(1, ens_n, b_start, 0, unroll=True)
    g_start(1, 0)
    lax.fori_loop(1, ens_n, b_wait, 0)

    spans = ((0, 1), (1, nb - 1))

    def c_copy(part, slot, peer, turn_at):
        first, count = spans[part]
        return pltpu.make_async_remote_copy(
            src_ref=c_src.at[pl.ds(first, count)],
            dst_ref=arrived.at[
                pl.ds(first, count), :, pl.ds(pl.multiple_of(slot * ens_n, ens_n), ens_n), :
            ],
            send_sem=c_send.at[part * dom_n + turn_at],
            recv_sem=c_recv.at[part * dom_n + slot],
            device_id=(e, peer),
            device_id_type=MESH,
        )

    def c_start(part):
        def one(i, carry):
            peer = lax.rem(d + i, dom_n)
            c_copy(part, d, peer, i).start()
            return carry

        lax.fori_loop(1, dom_n, one, 0, unroll=True)

    def c_wait(part):
        def one(i, carry):
            peer = lax.rem(d + i, dom_n)
            c_copy(part, peer, peer, i).wait_recv()
            return carry

        lax.fori_loop(1, dom_n, one, 0)

    c_start(0)
    c_start(1)
    g_wait(0, 0)
    g_start(0, 1)
    arrived[:, :, pl.ds(pl.multiple_of(d * ens_n, ens_n), ens_n), :] = c_src[...]
    for copy in halos:
        copy.wait_send()

    def sent_a(i, carry):
        a_copy(0, d, down, i).wait_send()
        return carry

    def sent_b(i, carry):
        b_copy(e, lax.rem(e + 1, ens_n), i).wait_send()
        return carry

    lax.fori_loop(1, dom_n, sent_a, 0, unroll=True)
    lax.fori_loop(1, ens_n, sent_b, 0, unroll=True)
    c_wait(0)
    g_wait(1, 0)
    g_start(1, 1)

    def in_order(b):
        columns = [
            jnp.concatenate(
                [arrived.at[b, p][pl.ds(k, mem_loc, stride=ens_n), :] for k in range(ens_n)], axis=0
            )
            for p in range(parts)
        ]
        return jnp.concatenate(columns, axis=1)

    eye = (
        lax.broadcasted_iota(jnp.int32, (members, members), 0)
        == lax.broadcasted_iota(jnp.int32, (members, members), 1)
    ).astype(jnp.float32)
    scale = 1.0 / (members - 1.0)
    low = members + PAD

    def analyse(observed, b):
        ybar = jnp.sum(observed, axis=0, keepdims=True) * (1.0 / members)
        rs = 1.0 / jnp.sqrt(var[pl.ds(b, 1), :])
        anom = (observed - ybar) * rs
        innov = (obs[pl.ds(b, 1), :] - ybar) * rs
        left = split3(jnp.concatenate([anom, jnp.broadcast_to(innov, (PAD, nob))], axis=0))
        both = dot6(left, [piece[:members] for piece in left], True) * scale
        gram = both[:members]
        z = both[members:]
        size = 1.001 * jnp.sqrt(jnp.sum(gram * gram, keepdims=True))
        alpha = 2.0 / (2.0 + size)
        r = size / (2.0 + size)
        k_mat = eye + gram
        gram_s[...] = k_mat
        err = eye - alpha * k_mat
        a = 2.0 / (2.0 - r * r)
        first = a * alpha
        pair[:members] = first * (eye + err)
        hi, lo = split2(jnp.concatenate([z, err], axis=0))
        prod = dot3((hi, lo), (hi[PAD:], lo[PAD:]))
        pair[members:low] = first * (z + prod[:PAD])
        pair[low:] = a * prod[PAD:] - (a - 1.0) * eye

        def advance(r, held, prod):
            a = 2.0 / (2.0 - r * r)
            pair[:low] = a * (held[:low] + prod[:low])
            pair[low:] = a * prod[low:] - (a - 1.0) * eye
            return a - 1.0

        def step(i, r):
            held = pair[...]
            hi, lo = split2(held)
            return advance(r, held, dot3((hi, lo), (hi[low:], lo[low:])))

        serve(b)
        r = lax.fori_loop(0, 6, step, a - 1.0)
        a = 2.0 / (2.0 - r * r)
        x = pair[:low]
        x = a * (x + dot3(split2(x), split2(pair[low:])))
        r = a - 1.0
        a = 2.0 / (2.0 - r * r)
        k_parts = split3(gram_s[...])
        x2 = split2(x)
        rest = eye - dot3(k_parts[:2], (x2[0][:members], x2[1][:members]))
        x = a * (x + dot3(x2, split2(rest)))
        rest = eye - dot6(k_parts, split3(x[:members]))
        x = x + dot3(split2(x), split2(rest))
        want = (lax.broadcasted_iota(jnp.int32, (low, 1), 0) < members).astype(jnp.float32)
        return x + (want - jnp.sum(x, axis=1, keepdims=True)) * (1.0 / members)

    def update(x, columns):
        prod = dot3(x, split2(columns))
        return 0.5 * (columns + prod[:members]) + prod[members : members + 1]

    prior[0] = in_order(0)

    def serve(b):
        part = lax.rem(b, 2)
        step = 2 + lax.div(b, 2)
        g_wait(part, step - 1)
        for way in (0, 1):

            @pl.when((b < 2) | (part == way))
            def _():
                g_copy(way, part, step, False).start()

    rows = pl.ds(pl.multiple_of(e * mem_loc, mem_loc), mem_loc)

    def batch(b, carry):
        x = analyse(prior[b], b)
        x2 = split2(x)

        @pl.when(b == 0)
        def _():
            total[...] = 0.5 * (eye + x[:members]) + x[members : members + 1]
            c_wait(1)
            for later in range(1, nb):
                prior[later] = in_order(later)

        def later_one(later, carry):
            prior[later] = update(x2, prior[later])
            return carry

        lax.fori_loop(b + 1, nb, later_one, 0)

        @pl.when((b > 0) & (b < nb - 1))
        def _():
            total[...] = update(x2, total[...])

        @pl.when(b == nb - 1)
        def _():
            pair[:low] = x
            thin = jnp.concatenate([pair[rows, :], x[members:]], axis=0)
            prod = dot3(split2(thin), split2(total[...]))
            t_own[...] = (
                0.5 * (total[rows, :] + prod[:mem_loc]) + prod[mem_loc : mem_loc + 1]
            )

        return carry

    lax.fori_loop(0, nb, batch, 0)
    g_copy(0, 0, 3, True).wait_recv()

    hi, lo = split2(t_own[...])
    both = jnp.concatenate([hi, lo], axis=0)

    def apply(i, carry):
        pieces = [
            jnp.concatenate(
                [
                    full[k, pl.ds(pl.multiple_of((2 * i + j) * mem_loc, mem_loc), mem_loc), :]
                    for k in range(ens_n)
                ],
                axis=0,
            )
            for j in range(2)
        ]
        x_hi, x_lo = split2(jnp.concatenate(pieces, axis=1))
        one = bdot(both, x_hi)
        res = one[:mem_loc] + one[mem_loc:] + bdot(hi, x_lo)
        out[pl.ds(2 * i, mem_loc, stride=rows_dev), :] = res[:, :cols]
        out[pl.ds(2 * i + 1, mem_loc, stride=rows_dev), :] = res[:, cols:]
        return carry

    lax.fori_loop(0, rows_dev // 4, apply, 0, unroll=4)
    g_copy(1, 1, 3, True).wait_recv()
    lax.fori_loop(rows_dev // 4, rows_dev // 2, apply, 0, unroll=4)

    for way in (0, 1):
        for part in (0, 1):
            for step in range(4 if way == part else 3):
                g_copy(way, part, step, False).wait_send()

    def sent_c(i, carry):
        c_copy(0, d, down, i).wait_send()
        c_copy(1, d, down, i).wait_send()
        return carry

    lax.fori_loop(1, dom_n, sent_c, 0, unroll=True)


def on_device(mesh_shape, state, row_c, col_c, diff, obs, var, off, owners):
    ens_n, dom_n = mesh_shape
    mem_loc, rows_dev, cols = state.shape
    members = mem_loc * ens_n
    nb, nob = obs.shape
    high = rows_dev + 2 * HALO
    f32 = jnp.float32
    sem = pltpu.SemaphoreType.DMA
    assert ens_n == 8 and nb == 4
    hbm = pl.BlockSpec(memory_space=pl.ANY)
    vmem = pl.BlockSpec(memory_space=pltpu.VMEM)
    result = pl.pallas_call(
        kernel,
        out_shape=jax.ShapeDtypeStruct((mem_loc * rows_dev, cols), f32),
        in_specs=[hbm] * 8,
        out_specs=vmem,
        scratch_shapes=[
            pltpu.VMEM((mem_loc, high, cols), f32),
            pltpu.VMEM((3, high, cols), f32),
            pltpu.VMEM((high * mem_loc, cols), f32),
            pltpu.VMEM((high * mem_loc, cols), f32),
            pltpu.VMEM((4, high, cols), f32),
            pltpu.VMEM((ens_n, rows_dev * mem_loc, cols), f32),
            pltpu.VMEM((nb, nob), f32),
            pltpu.VMEM((nb, nob), f32),
            pltpu.VMEM((nb, nob), jnp.int32),
            pltpu.SMEM((nb,), jnp.int32),
            pltpu.VMEM((cols, nob), jnp.bfloat16),
            pltpu.VMEM((rows_dev, nob), f32),
            pltpu.VMEM((mem_loc, nob), f32),
            pltpu.VMEM((dom_n, 1, nob), f32),
            pltpu.VMEM((nb, nob // cols, 1, cols), f32),
            pltpu.VMEM((nb, nob // cols, ens_n, cols), f32),
            pltpu.VMEM((nb, nob // cols, members, cols), f32),
            pltpu.VMEM((nb, members, nob), f32),
            pltpu.VMEM((2 * members + PAD, members), f32),
            pltpu.VMEM((members, members), f32),
            pltpu.VMEM((members, members), f32),
            pltpu.VMEM((mem_loc, members), f32),
            sem((8,)),
            sem((8,)),
            sem((8,)),
            sem((dom_n,)),
            sem((dom_n,)),
            sem((ens_n,)),
            sem((ens_n,)),
            sem((2 * dom_n,)),
            sem((2 * dom_n,)),
            sem((16,)),
            sem((16,)),
        ],
        compiler_params=pltpu.CompilerParams(
            collective_id=0, has_side_effects=True, vmem_limit_bytes=60 * 1024 * 1024
        ),
    )(state, row_c, col_c, diff, obs, var, off, owners)
    return result.reshape(mem_loc, rows_dev, cols)


def solution(mesh):
    sizes = (mesh.shape["ens"], mesh.shape["dom"])
    return jax.shard_map(
        functools.partial(on_device, sizes),
        mesh=mesh,
        in_specs=(
            P("ens", "dom", None),
            P("dom", None),
            P("dom", None),
            P("dom", None),
            P(),
            P(),
            P(),
            P(),
        ),
        out_specs=P("ens", "dom", None),
        check_vma=False,
    )
```

```python
import functools

import jax
import jax.numpy as jnp
from jax import lax
from jax.experimental import pallas as pl
from jax.experimental.pallas import tpu as pltpu
from jax.sharding import PartitionSpec as P

MESH = pl.DeviceIdType.MESH
FSTEPS = 4
HALO = 8
PAD = 8


def split2(x):
    hi = x.astype(jnp.bfloat16)
    lo = (x - hi.astype(jnp.float32)).astype(jnp.bfloat16)
    return hi, lo


def dot6(a, b, transposed=False):
    a_hi, a_mid, a_lo = a
    b_hi, b_mid, b_lo = b
    axis = 1 if transposed else 0
    left = jnp.concatenate([a_hi, a_mid, a_hi, a_mid, a_lo, a_hi], axis=1)
    right = jnp.concatenate([b_hi, b_hi, b_mid, b_mid, b_hi, b_lo], axis=axis)
    return lax.dot_general(
        left, right, (((1,), (axis,)), ((), ())), preferred_element_type=jnp.float32
    )


def split3(x):
    hi = x.astype(jnp.bfloat16)
    rest = x - hi.astype(jnp.float32)
    mid = rest.astype(jnp.bfloat16)
    lo = (rest - mid.astype(jnp.float32)).astype(jnp.bfloat16)
    return hi, mid, lo


def bdot(a, b):
    return jnp.dot(a, b, preferred_element_type=jnp.float32)


def dot3(a, b):
    a_hi, a_lo = a
    b_hi, b_lo = b
    return bdot(
        jnp.concatenate([a_hi, a_lo, a_hi], axis=1), jnp.concatenate([b_hi, b_hi, b_lo], axis=0)
    )


def kernel(
    state, row_c, col_c, diff, obs_in, var_in, off_in, own_in, out,
    ext, cext, cells, other, weight, full, obs, var, off, own, lane_hot, row_hot, hx, a_in, b_out, c_src,
    arrived, prior, pair, gram_s, total, t_own,
    load_sem, h_send, h_recv, a_send, a_recv, b_send, b_recv, c_send, c_recv, g_send, g_recv,
):
    ens_n = lax.axis_size("ens")
    dom_n = lax.axis_size("dom")
    e = lax.axis_index("ens")
    d = lax.axis_index("dom")
    mem_loc, rows_dev, cols = state.shape
    members = mem_loc * ens_n
    nb, nob = obs.shape
    parts = nob // cols
    high = rows_dev + 2 * HALO

    inner = pl.ds(HALO, rows_dev)
    moves = [(state, ext.at[:, inner, :])]
    moves += [(coef, cext.at[i, inner, :]) for i, coef in enumerate((row_c, col_c, diff))]
    moves += [(obs_in, obs), (var_in, var), (off_in, off), (own_in, own)]
    loads = [pltpu.make_async_copy(src, dst, load_sem.at[i]) for i, (src, dst) in enumerate(moves)]
    for copy in loads:
        copy.start()

    barrier = pltpu.get_barrier_semaphore()

    def greet_dom(i, carry):
        pl.semaphore_signal(
            barrier, inc=1, device_id=(e, lax.rem(d + i, dom_n)), device_id_type=MESH
        )
        return carry

    def greet_ens(i, carry):
        pl.semaphore_signal(
            barrier, inc=1, device_id=(lax.rem(e + i, ens_n), d), device_id_type=MESH
        )
        return carry

    lax.fori_loop(1, dom_n, greet_dom, 0)
    lax.fori_loop(1, ens_n, greet_ens, 0)
    for copy in loads:
        copy.wait()
    pl.semaphore_wait(barrier, dom_n - 1 + ens_n - 1)

    down = lax.rem(d + 1, dom_n)
    up = lax.rem(d + dom_n - 1, dom_n)
    halos = []
    for way, (src_row, dst_row, peer) in enumerate(
        ((rows_dev - HALO, 0, down), (0, HALO + rows_dev, up))
    ):
        halos.append(
            pltpu.make_async_remote_copy(
                src_ref=ext.at[:, pl.ds(HALO + src_row, HALO), :],
                dst_ref=ext.at[:, pl.ds(dst_row, HALO), :],
                send_sem=h_send.at[way * 4],
                recv_sem=h_recv.at[way * 4],
                device_id=(e, peer),
                device_id_type=MESH,
            )
        )
        for i in range(3):
            halos.append(
                pltpu.make_async_remote_copy(
                    src_ref=cext.at[i, pl.ds(HALO + src_row, HALO), :],
                    dst_ref=cext.at[i, pl.ds(dst_row, HALO), :],
                    send_sem=h_send.at[way * 4 + 1 + i],
                    recv_sem=h_recv.at[way * 4 + 1 + i],
                    device_id=(e, peer),
                    device_id_type=MESH,
                )
            )
    for copy in halos:
        copy.start()

    offs = jnp.zeros((1, nob), jnp.int32)
    for b in range(nb):
        offs = offs + off[pl.ds(b, 1), :] * (own[b] == d).astype(jnp.int32)
    lane_of = lax.rem(offs, cols)
    row_of = lax.div(offs, cols)
    lane_hot[...] = (
        lax.broadcasted_iota(jnp.int32, (cols, nob), 0) == lane_of
    ).astype(jnp.float32).astype(jnp.bfloat16)
    row_hot[...] = (
        lax.broadcasted_iota(jnp.int32, (rows_dev, nob), 0) == row_of
    ).astype(jnp.float32)

    def turn(first, count):
        def one(m, carry):
            cells[pl.ds(first * mem_loc + m, count, stride=mem_loc), :] = ext[m, pl.ds(first, count), :]
            return carry

        lax.fori_loop(0, mem_loc, one, 0, unroll=4)

    turn(HALO, rows_dev)
    for copy in halos:
        copy.wait_recv()
    turn(0, HALO)
    turn(HALO + rows_dev, HALO)
    rc, cc, df = cext[0], cext[1], cext[2]
    weight[0] = 1.0 - rc - cc - 4.0 * df
    weight[1] = rc + df
    weight[2] = cc + df
    weight[3] = df

    def at_row(r):
        return pl.ds(pl.multiple_of(r * mem_loc, mem_loc), mem_loc)

    def coef(i, r):
        return jnp.broadcast_to(weight[i, pl.ds(r, 1), :], (mem_loc, cols))

    for step in range(FSTEPS):
        first = HALO - (FSTEPS - 1 - step)
        last = HALO + rows_dev + (FSTEPS - 1 - step)

        src, dst = (cells, other) if step % 2 == 0 else (other, cells)

        def one(r, carry, step=step, src=src, dst=dst):
            above, here = carry
            below = src[at_row(r + 1), :]
            left = pltpu.roll(here, 1, 1)
            right = pltpu.roll(here, cols - 1, 1)
            fresh = (
                coef(0, r) * here
                + coef(1, r) * above
                + coef(2, r) * left
                + coef(3, r) * (below + right)
            )
            if step < FSTEPS - 1:
                dst[at_row(r), :] = fresh
            else:
                full[e, at_row(r - HALO), :] = fresh
            return here, below

        lax.fori_loop(
            first,
            last,
            one,
            (src[at_row(first - 1), :], src[at_row(first), :]),
            unroll=(last - first) // 2,
        )

    half = rows_dev * mem_loc // 2

    def g_copy(way, part, step, arriving):
        shift = step + 1 if arriving else step
        block = lax.rem(e - shift + ens_n, ens_n) if way == 0 else lax.rem(e + shift, ens_n)
        peer = lax.rem(e + 1, ens_n) if way == 0 else lax.rem(e + ens_n - 1, ens_n)
        where = full.at[block, pl.ds(pl.multiple_of(part * half, half), half), :]
        slot = (way * 2 + part) * 4 + step
        return pltpu.make_async_remote_copy(
            src_ref=where,
            dst_ref=where,
            send_sem=g_send.at[slot],
            recv_sem=g_recv.at[slot],
            device_id=(peer, d),
            device_id_type=MESH,
        )

    def g_start(part, step):
        for way in (0, 1):
            g_copy(way, part, step, False).start()

    def g_wait(part, step):
        for way in (0, 1):
            g_copy(way, part, step, True).wait_recv()

    g_start(0, 0)

    rows_once = 4

    def pick(i, acc):
        block = pl.ds(pl.multiple_of(i * rows_once * mem_loc, rows_once * mem_loc), rows_once * mem_loc)
        hi, lo = split2(full[e, block, :])
        hot = lane_hot[...]
        picked = bdot(hi, hot) + bdot(lo, hot)
        for j in range(rows_once):
            acc = acc + picked[j * mem_loc : (j + 1) * mem_loc] * row_hot[
                pl.ds(i * rows_once + j, 1), :
            ]
        return acc

    hx[...] = lax.fori_loop(
        0, rows_dev // rows_once, pick, jnp.zeros((mem_loc, nob), jnp.float32), unroll=2
    )

    def a_copy(src, dst, peer, turn_at):
        return pltpu.make_async_remote_copy(
            src_ref=hx.at[pl.ds(src, 1), :],
            dst_ref=a_in.at[dst],
            send_sem=a_send.at[turn_at],
            recv_sem=a_recv.at[dst],
            device_id=(e, peer),
            device_id_type=MESH,
        )

    def a_start(i, carry):
        peer = lax.rem(d + i, dom_n)
        a_copy(peer, d, peer, i).start()
        return carry

    def a_wait(i, carry):
        peer = lax.rem(d + i, dom_n)
        a_copy(peer, peer, peer, i).wait_recv()
        return carry

    lax.fori_loop(1, dom_n, a_start, 0, unroll=True)
    a_in[d] = hx[pl.ds(d, 1), :]

    lax.fori_loop(1, dom_n, a_wait, 0, unroll=True)

    for b in range(nb):
        row = a_in[own[b]]
        for p in range(parts):
            piece = row[:, p * cols : (p + 1) * cols]
            b_out[b, p] = piece
            c_src[b, p, pl.ds(e, 1), :] = piece

    def b_copy(slot, peer, turn_at):
        return pltpu.make_async_remote_copy(
            src_ref=b_out,
            dst_ref=c_src.at[:, :, pl.ds(slot, 1), :],
            send_sem=b_send.at[turn_at],
            recv_sem=b_recv.at[slot],
            device_id=(peer, d),
            device_id_type=MESH,
        )

    def b_start(i, carry):
        peer = lax.rem(e + i, ens_n)
        b_copy(e, peer, i).start()
        return carry

    def b_wait(i, carry):
        peer = lax.rem(e + i, ens_n)
        b_copy(peer, peer, i).wait_recv()
        return carry

    lax.fori_loop(1, ens_n, b_start, 0, unroll=True)
    g_start(1, 0)
    lax.fori_loop(1, ens_n, b_wait, 0, unroll=True)

    spans = ((0, 1), (1, nb - 1))

    def c_copy(part, slot, peer, turn_at):
        first, count = spans[part]
        return pltpu.make_async_remote_copy(
            src_ref=c_src.at[pl.ds(first, count)],
            dst_ref=arrived.at[
                pl.ds(first, count), :, pl.ds(pl.multiple_of(slot * ens_n, ens_n), ens_n), :
            ],
            send_sem=c_send.at[part * dom_n + turn_at],
            recv_sem=c_recv.at[part * dom_n + slot],
            device_id=(e, peer),
            device_id_type=MESH,
        )

    def c_start(part):
        def one(i, carry):
            peer = lax.rem(d + i, dom_n)
            c_copy(part, d, peer, i).start()
            return carry

        lax.fori_loop(1, dom_n, one, 0, unroll=True)

    def c_wait(part):
        def one(i, carry):
            peer = lax.rem(d + i, dom_n)
            c_copy(part, peer, peer, i).wait_recv()
            return carry

        lax.fori_loop(1, dom_n, one, 0, unroll=True)

    c_start(0)
    c_start(1)
    g_wait(0, 0)
    g_start(0, 1)
    arrived[:, :, pl.ds(pl.multiple_of(d * ens_n, ens_n), ens_n), :] = c_src[...]
    for copy in halos:
        copy.wait_send()

    def sent_a(i, carry):
        a_copy(0, d, down, i).wait_send()
        return carry

    def sent_b(i, carry):
        b_copy(e, lax.rem(e + 1, ens_n), i).wait_send()
        return carry

    lax.fori_loop(1, dom_n, sent_a, 0, unroll=True)
    lax.fori_loop(1, ens_n, sent_b, 0, unroll=True)
    c_wait(0)
    g_wait(1, 0)
    g_start(1, 1)

    def in_order(b):
        columns = [
            jnp.concatenate(
                [arrived.at[b, p][pl.ds(k, mem_loc, stride=ens_n), :] for k in range(ens_n)], axis=0
            )
            for p in range(parts)
        ]
        return jnp.concatenate(columns, axis=1)

    eye = (
        lax.broadcasted_iota(jnp.int32, (members, members), 0)
        == lax.broadcasted_iota(jnp.int32, (members, members), 1)
    ).astype(jnp.float32)
    scale = 1.0 / (members - 1.0)
    low = members + PAD

    def analyse(observed, b):
        ybar = jnp.sum(observed, axis=0, keepdims=True) * (1.0 / members)
        rs = 1.0 / jnp.sqrt(var[pl.ds(b, 1), :])
        anom = (observed - ybar) * rs
        innov = (obs[pl.ds(b, 1), :] - ybar) * rs
        left = split3(jnp.concatenate([anom, jnp.broadcast_to(innov, (PAD, nob))], axis=0))
        both = dot6(left, [piece[:members] for piece in left], True) * scale
        gram = both[:members]
        z = both[members:]
        size = 1.001 * jnp.sqrt(jnp.sum(gram * gram, keepdims=True))
        alpha = 2.0 / (2.0 + size)
        r = size / (2.0 + size)
        k_mat = eye + gram
        gram_s[...] = k_mat
        err = eye - alpha * k_mat
        a = 2.0 / (2.0 - r * r)
        first = a * alpha
        pair[:members] = first * (eye + err)
        hi, lo = split2(jnp.concatenate([z, err], axis=0))
        prod = dot3((hi, lo), (hi[PAD:], lo[PAD:]))
        pair[members:low] = first * (z + prod[:PAD])
        pair[low:] = a * prod[PAD:] - (a - 1.0) * eye

        def advance(r, held, prod):
            a = 2.0 / (2.0 - r * r)
            pair[:low] = a * (held[:low] + prod[:low])
            pair[low:] = a * prod[low:] - (a - 1.0) * eye
            return a - 1.0

        def step(i, r):
            held = pair[...]
            hi, lo = split2(held)
            return advance(r, held, dot3((hi, lo), (hi[low:], lo[low:])))

        serve(b)
        r = lax.fori_loop(0, 6, step, a - 1.0)
        a = 2.0 / (2.0 - r * r)
        x = pair[:low]
        x = a * (x + dot3(split2(x), split2(pair[low:])))
        r = a - 1.0
        a = 2.0 / (2.0 - r * r)
        k_parts = split3(gram_s[...])
        x2 = split2(x)
        rest = eye - dot3(k_parts[:2], (x2[0][:members], x2[1][:members]))
        x = a * (x + dot3(x2, split2(rest)))
        rest = eye - dot6(k_parts, split3(x[:members]))
        x = x + dot3(split2(x), split2(rest))
        want = (lax.broadcasted_iota(jnp.int32, (low, 1), 0) < members).astype(jnp.float32)
        return x + (want - jnp.sum(x, axis=1, keepdims=True)) * (1.0 / members)

    def update(x, columns):
        prod = dot3(x, split2(columns))
        return 0.5 * (columns + prod[:members]) + prod[members : members + 1]

    prior[0] = in_order(0)

    def serve(b):
        part = lax.rem(b, 2)
        step = 2 + lax.div(b, 2)
        g_wait(part, step - 1)
        for way in (0, 1):

            @pl.when((b < 2) | (part == way))
            def _():
                g_copy(way, part, step, False).start()

    rows = pl.ds(pl.multiple_of(e * mem_loc, mem_loc), mem_loc)

    def batch(b, carry):
        x = analyse(prior[b], b)
        x2 = split2(x)

        @pl.when(b == 0)
        def _():
            total[...] = 0.5 * (eye + x[:members]) + x[members : members + 1]
            c_wait(1)
            for later in range(1, nb):
                prior[later] = in_order(later)

        def later_one(later, carry):
            prior[later] = update(x2, prior[later])
            return carry

        lax.fori_loop(b + 1, nb, later_one, 0)

        @pl.when((b > 0) & (b < nb - 1))
        def _():
            total[...] = update(x2, total[...])

        @pl.when(b == nb - 1)
        def _():
            pair[:low] = x
            thin = jnp.concatenate([pair[rows, :], x[members:]], axis=0)
            prod = dot3(split2(thin), split2(total[...]))
            t_own[...] = (
                0.5 * (total[rows, :] + prod[:mem_loc]) + prod[mem_loc : mem_loc + 1]
            )

        return carry

    lax.fori_loop(0, nb, batch, 0)
    g_copy(0, 0, 3, True).wait_recv()

    hi, lo = split2(t_own[...])
    both = jnp.concatenate([hi, lo], axis=0)

    def apply(i, carry):
        pieces = [
            jnp.concatenate(
                [
                    full[k, pl.ds(pl.multiple_of((2 * i + j) * mem_loc, mem_loc), mem_loc), :]
                    for k in range(ens_n)
                ],
                axis=0,
            )
            for j in range(2)
        ]
        x_hi, x_lo = split2(jnp.concatenate(pieces, axis=1))
        one = bdot(both, x_hi)
        res = one[:mem_loc] + one[mem_loc:] + bdot(hi, x_lo)
        out[pl.ds(2 * i, mem_loc, stride=rows_dev), :] = res[:, :cols]
        out[pl.ds(2 * i + 1, mem_loc, stride=rows_dev), :] = res[:, cols:]
        return carry

    lax.fori_loop(0, rows_dev // 4, apply, 0, unroll=4)
    g_copy(1, 1, 3, True).wait_recv()
    lax.fori_loop(rows_dev // 4, rows_dev // 2, apply, 0, unroll=4)

    for way in (0, 1):
        for part in (0, 1):
            for step in range(4 if way == part else 3):
                g_copy(way, part, step, False).wait_send()

    def sent_c(i, carry):
        c_copy(0, d, down, i).wait_send()
        c_copy(1, d, down, i).wait_send()
        return carry

    lax.fori_loop(1, dom_n, sent_c, 0, unroll=True)


def on_device(mesh_shape, state, row_c, col_c, diff, obs, var, off, owners):
    ens_n, dom_n = mesh_shape
    mem_loc, rows_dev, cols = state.shape
    members = mem_loc * ens_n
    nb, nob = obs.shape
    high = rows_dev + 2 * HALO
    f32 = jnp.float32
    sem = pltpu.SemaphoreType.DMA
    assert ens_n == 8 and nb == 4
    hbm = pl.BlockSpec(memory_space=pl.ANY)
    vmem = pl.BlockSpec(memory_space=pltpu.VMEM)
    result = pl.pallas_call(
        kernel,
        out_shape=jax.ShapeDtypeStruct((mem_loc * rows_dev, cols), f32),
        in_specs=[hbm] * 8,
        out_specs=vmem,
        scratch_shapes=[
            pltpu.VMEM((mem_loc, high, cols), f32),
            pltpu.VMEM((3, high, cols), f32),
            pltpu.VMEM((high * mem_loc, cols), f32),
            pltpu.VMEM((high * mem_loc, cols), f32),
            pltpu.VMEM((4, high, cols), f32),
            pltpu.VMEM((ens_n, rows_dev * mem_loc, cols), f32),
            pltpu.VMEM((nb, nob), f32),
            pltpu.VMEM((nb, nob), f32),
            pltpu.VMEM((nb, nob), jnp.int32),
            pltpu.SMEM((nb,), jnp.int32),
            pltpu.VMEM((cols, nob), jnp.bfloat16),
            pltpu.VMEM((rows_dev, nob), f32),
            pltpu.VMEM((mem_loc, nob), f32),
            pltpu.VMEM((dom_n, 1, nob), f32),
            pltpu.VMEM((nb, nob // cols, 1, cols), f32),
            pltpu.VMEM((nb, nob // cols, ens_n, cols), f32),
            pltpu.VMEM((nb, nob // cols, members, cols), f32),
            pltpu.VMEM((nb, members, nob), f32),
            pltpu.VMEM((2 * members + PAD, members), f32),
            pltpu.VMEM((members, members), f32),
            pltpu.VMEM((members, members), f32),
            pltpu.VMEM((mem_loc, members), f32),
            sem((8,)),
            sem((8,)),
            sem((8,)),
            sem((dom_n,)),
            sem((dom_n,)),
            sem((ens_n,)),
            sem((ens_n,)),
            sem((2 * dom_n,)),
            sem((2 * dom_n,)),
            sem((16,)),
            sem((16,)),
        ],
        compiler_params=pltpu.CompilerParams(
            collective_id=0, has_side_effects=True, vmem_limit_bytes=60 * 1024 * 1024
        ),
    )(state, row_c, col_c, diff, obs, var, off, owners)
    return result.reshape(mem_loc, rows_dev, cols)


def solution(mesh):
    sizes = (mesh.shape["ens"], mesh.shape["dom"])
    return jax.shard_map(
        functools.partial(on_device, sizes),
        mesh=mesh,
        in_specs=(
            P("ens", "dom", None),
            P("dom", None),
            P("dom", None),
            P("dom", None),
            P(),
            P(),
            P(),
            P(),
        ),
        out_specs=P("ens", "dom", None),
        check_vma=False,
    )
```
